512 devices in a mesh: depth: 16 (over y, core), cam: 32 (over x, z).
Axes of the slice: x: 4, y: 8, z: 8, core: 2. Of those that a mesh axis runs over, the one named last changes fastest.
Arguments:
- block_rays: int32 [16, 32, 32], P('depth', 'cam'), may hold values from -1 to 127, as said below
- block_offsets: int32 [16, 32, 32], P('depth', 'cam'), may hold values from 0 to 255
- view_order: int32 [32], P('cam'), may hold values from 0 to 1
- ray_frames: float32 [32, 6, 128], P('cam'), may hold values from -6 to 6
- target: float32 [32, 128, 64], P('cam'), may hold values from -3 to 3
- enc_freq: float32 [16, 3, 64], P('depth'), may hold values from -32 to 32
- w_in: bfloat16 [16, 128, 256], P('depth'), may hold values from -0.5 to 0.5
- b_in: float32 [16, 256], P('depth'), may hold values from -3 to 3
- w_mid: bfloat16 [16, 256, 256], P('depth'), may hold values from -0.375 to 0.375
- b_mid: float32 [16, 256], P('depth'), may hold values from -3 to 3
- w_feat: bfloat16 [16, 256, 64], P('depth'), may hold values from -0.375 to 0.375
- w_dens: bfloat16 [16, 256], P('depth'), may hold values from -0.375 to 0.375
Outputs:
- pixels: float32 [32, 128, 64], P('cam', 'depth')
- grad_w_in: float32 [16, 128, 256], P('depth', 'cam')
- grad_b_in: float32 [16, 256], P('depth', 'cam')
- grad_w_mid: float32 [16, 256, 256], P('depth', 'cam')
- grad_b_mid: float32 [16, 256], P('depth', 'cam')
- grad_w_feat: float32 [16, 256, 64], P('depth', 'cam')
- grad_w_dens: float32 [16, 256], P('depth', 'cam')
The draws below stay inside these ranges and needn't reach their ends.
Inputs may be any that keep to these rules, and one draw needn't show every extreme that they name: `block_rays`: for each region and batch the used slots come first and hold distinct ray numbers of that batch; later slots hold -1. A region's slots over all batches hold at most 256 ray numbers; in every draw some region holds exactly that many, with one batch in it whose 32 slots are all used.
All inputs are finite; a program needn't handle non-finite values.
Results may differ from the reference program's by a relative error of at most 0.011.
Values sent between devices are 32-bit elements; how exact they have to be, the bound alone decides.
No kernel may reach another device: no remote copies, remote signals or barrier semaphores. Data moves between devices by JAX's collectives and lax.ppermute only.
A program may use at most 64 MiB of HBM per device.

```python
import jax
import jax.numpy as jnp
from jax import lax

HID = 256
ENC = 128
FEAT = 64
BLK = 128
OFFS = 256
RAYS = 128
CAP = 32
REGIONS = 16
BATCHES = 32


def region_counts(subkey, is_full):
    quarter = CAP // 4
    subkeys = jax.random.split(subkey, 3)
    ranking = jax.random.permutation(subkeys[0], BATCHES)
    shifts = jax.random.randint(subkeys[1], ((BATCHES - 4) // 2,), -quarter, quarter + 1)
    paired = jnp.stack([quarter + shifts, quarter - shifts], axis=1).reshape(-1)
    values = jnp.concatenate([jnp.full((1,), CAP, jnp.int32), jnp.zeros((3,), jnp.int32), paired.astype(jnp.int32)])
    counts = jnp.zeros((BATCHES,), jnp.int32).at[ranking].set(values)
    ceiling = jnp.where(is_full, CAP, jax.random.randint(subkeys[2], (), quarter, CAP + 1))
    return jnp.minimum(counts, ceiling)


def choose_rays(subkey):
    return jax.random.permutation(subkey, RAYS)[:CAP]


def draw_block_rays(key, part):
    subkeys = jax.random.split(jax.random.fold_in(key, 11), REGIONS + 2)
    full_region = jax.random.randint(subkeys[0], (), 0, REGIONS)
    counts = jax.vmap(region_counts)(subkeys[2:], jnp.arange(REGIONS) == full_region)
    ray_keys = jax.random.split(subkeys[1], REGIONS * BATCHES)
    chosen = jax.vmap(choose_rays)(ray_keys).reshape(REGIONS, BATCHES, CAP)
    occupied = jnp.arange(CAP)[None, None, :] < counts[:, :, None]
    return jnp.where(occupied, chosen, -1).astype(jnp.int32)


def place_ends(result, key, least, high):
    longest = result.shape.index(max(result.shape))
    spots = []
    for shift in (0, 1):
        where = [jax.random.randint(jax.random.fold_in(key, axis), (), 0, length) for axis, length in enumerate(result.shape)]
        where[longest] = (where[longest] + shift) % result.shape[longest]
        spots.append(tuple(where))
    return result.at[spots[0]].set(least).at[spots[1]].set(high)


def level_of(rng, extent, shards, least, top_value):
    def one(position, parts):
        steps = jax.random.uniform(jax.random.fold_in(jax.random.fold_in(rng, 6), position), (parts,), jnp.float32, least / len(shards), top_value / len(shards))
        return jnp.repeat(jnp.exp(steps), extent[position] // parts).reshape((-1,) + (1,) * (len(extent) - position - 1))

    factor_of = one(*shards[0])
    for cut in shards[1:]:
        factor_of = factor_of * one(*cut)
    return factor_of


def scatter_about(stream_key, shape, deviation, bound, cuts=(), kind=jnp.bfloat16):
    entries = jax.random.normal(stream_key, shape, jnp.float32) * deviation
    if len(cuts) > 0:
        entries = level_of(stream_key, shape, cuts, -0.22, 0.18) * entries
    return jnp.clip(entries, min=-bound, max=bound).astype(kind)


def setup_inputs(seed: int = 0) -> dict:
    key_list = jax.random.split(jax.random.key(seed), 13)
    return {
        "block_rays": draw_block_rays(jax.random.fold_in(key_list[12], 71), 0),
        "block_offsets": place_ends(jax.random.randint(key_list[1], (REGIONS, BATCHES, CAP), 0, OFFS), jax.random.fold_in(key_list[1], 1), 0, OFFS - 1).astype(jnp.int32),
        "view_order": place_ends(jax.random.randint(key_list[2], (BATCHES,), 0, 2), jax.random.fold_in(key_list[2], 1), 0, 1).astype(jnp.int32),
        "ray_frames": scatter_about(key_list[3], (BATCHES, 6, RAYS), 1.0, 6.0, ((0, 32),), jnp.float32),
        "target": scatter_about(key_list[4], (BATCHES, RAYS, FEAT), 0.5, 3.0, ((0, 32),), jnp.float32),
        "enc_freq": scatter_about(key_list[5], (REGIONS, 3, ENC // 2), 6.0, 32.0, ((0, 16),), jnp.float32),
        "w_in": scatter_about(key_list[6], (REGIONS, ENC, HID), ENC ** -0.5, 0.5, ((0, 16),)),
        "b_in": scatter_about(key_list[7], (REGIONS, HID), 0.5, 3.0, ((0, 16),), jnp.float32),
        "w_mid": scatter_about(key_list[8], (REGIONS, HID, HID), HID ** -0.5, 0.375, ((0, 16),)),
        "b_mid": scatter_about(key_list[9], (REGIONS, HID), 0.5, 3.0, ((0, 16),), jnp.float32),
        "w_feat": scatter_about(key_list[10], (REGIONS, HID, FEAT), HID ** -0.5, 0.375, ((0, 16),)),
        "w_dens": scatter_about(key_list[11], (REGIONS, HID), HID ** -0.5, 0.375, ((0, 16),)),
    }


step_length = 1.0 / 64.0


def contract_rows(left, right):
    return lax.dot_general(left, right, (((0,), (0,)), ((), ())), preferred_element_type=jnp.float32)


def contract_cols(left, right):
    return lax.dot_general(left, right, (((1,), (1,)), ((), ())), preferred_element_type=jnp.float32)


def strict_upper(samples):
    rows_index = lax.broadcasted_iota(jnp.int32, (samples, samples), 0)
    cols_index = lax.broadcasted_iota(jnp.int32, (samples, samples), 1)
    return (rows_index < cols_index).astype(jnp.float32)


def block_forward(geometry, offsets, frequency, w_in, b_in, w_mid, b_mid, w_feat, w_dens):
    block_count = offsets.shape[0]
    samples = BLK
    positions = (offsets.astype(jnp.float32)[:, None] + jnp.arange(samples, dtype=jnp.float32)[None, :] + 0.5) * step_length
    phases = jnp.zeros((block_count * samples, frequency.shape[1]), jnp.float32)
    for component in range(3):
        coordinate = (geometry[component][:, None] + positions * geometry[component + 3][:, None]).reshape(-1)
        phases = phases + coordinate[:, None] * frequency[component][None, :]
    encoded = jnp.concatenate([jnp.sin(phases), jnp.cos(phases)], axis=1).astype(jnp.bfloat16)
    hidden_one = jax.nn.relu(jnp.dot(encoded, w_in, preferred_element_type=jnp.float32) + b_in).astype(jnp.bfloat16)
    hidden_two = jax.nn.relu(jnp.dot(hidden_one, w_mid, preferred_element_type=jnp.float32) + b_mid).astype(jnp.bfloat16)
    features = jnp.dot(hidden_two, w_feat, preferred_element_type=jnp.float32)
    dens_pre = jnp.dot(hidden_two, w_dens, preferred_element_type=jnp.float32)
    tau_step = (jax.nn.softplus(dens_pre) * step_length).reshape(block_count, samples)
    before = jnp.dot(tau_step, strict_upper(samples), precision=lax.Precision.HIGHEST)
    weights = jnp.exp(-before) * (-jnp.expm1(-tau_step))
    feature_grid = features.reshape(block_count, samples, features.shape[1])
    colour = jnp.einsum("bs,bsf->bf", weights, feature_grid, precision=lax.Precision.HIGHEST)
    through = jnp.exp(-(before[:, -1] + tau_step[:, -1]))
    stored = (encoded, hidden_one, hidden_two, feature_grid, dens_pre, tau_step, before, weights, through)
    return colour, through, stored


def block_backward(stored, d_colour, d_through, w_mid, w_feat, w_dens):
    encoded, hidden_one, hidden_two, feature_grid, dens_pre, tau_step, before, weights, through = stored
    projected = jnp.einsum("bsf,bf->bs", feature_grid, d_colour, precision=lax.Precision.HIGHEST)
    behind = jnp.dot(projected * weights, strict_upper(BLK).T, precision=lax.Precision.HIGHEST)
    d_tau = projected * jnp.exp(-(before + tau_step)) - behind - (d_through * through)[:, None]
    d_pre = ((d_tau * step_length).reshape(-1) * jax.nn.sigmoid(dens_pre)).astype(jnp.bfloat16)
    d_feat = (weights[:, :, None] * d_colour[:, None, :]).reshape(-1, d_colour.shape[1]).astype(jnp.bfloat16)
    grad_feat = contract_rows(hidden_two, d_feat)
    grad_dens = jnp.dot(d_pre, hidden_two, preferred_element_type=jnp.float32)
    d_two = contract_cols(d_feat, w_feat) + d_pre.astype(jnp.float32)[:, None] * w_dens.astype(jnp.float32)[None, :]
    d_two = jnp.where(hidden_two > 0, d_two, 0.0).astype(jnp.bfloat16)
    grad_mid = contract_rows(hidden_one, d_two)
    grad_bmid = jnp.sum(d_two.astype(jnp.float32), axis=0)
    d_one = jnp.where(hidden_one > 0, contract_cols(d_two, w_mid), 0.0).astype(jnp.bfloat16)
    grad_in = contract_rows(encoded, d_one)
    grad_bin = jnp.sum(d_one.astype(jnp.float32), axis=0)
    return grad_in, grad_bin, grad_mid, grad_bmid, grad_feat, grad_dens


def join_pairs(low_pair, high_pair, descending):
    low_colour, low_through = low_pair
    high_colour, high_through = high_pair
    rising = low_colour + low_through[..., None] * high_colour
    falling = high_colour + high_through[..., None] * low_colour
    return jnp.where(descending, falling, rising), low_through * high_through


def region_inputs(region, block_rays, block_offsets, ray_frames, kept_slots):
    capacity = block_rays.shape[2]
    flat_rays = block_rays[region].reshape(-1)
    ranking = jnp.argsort((flat_rays < 0).astype(jnp.int32), stable=True)[:kept_slots].astype(jnp.int32)
    batch_of = (ranking // capacity).astype(jnp.int32)
    ray_number = flat_rays[ranking]
    occupied = ray_number >= 0
    ray_index = jnp.maximum(ray_number, 0).astype(jnp.int32)
    geometry = ray_frames[batch_of, :, ray_index].T
    offsets = block_offsets[region].reshape(-1)[ranking]
    return batch_of, ray_number, occupied, ray_index, geometry, offsets


def reference(block_rays, block_offsets, view_order, ray_frames, target, enc_freq, w_in, b_in, w_mid, b_mid, w_feat, w_dens):
    regions, batches, capacity = block_rays.shape
    ray_total = target.shape[1]
    feature_count = target.shape[2]
    kept_slots = batches * (capacity // 4)
    descending = (view_order == 1)[:, None, None]

    def params_of(region):
        return (enc_freq[region], w_in[region], b_in[region], w_mid[region], b_mid[region], w_feat[region], w_dens[region])

    def forward_region(region):
        batch_of, ray_number, occupied, ray_index, geometry, offsets = region_inputs(region, block_rays, block_offsets, ray_frames, kept_slots)
        colour, through, stored = block_forward(geometry, offsets, *params_of(region))
        slot_ray = jnp.where(occupied, ray_number, ray_total).astype(jnp.int32)
        own_colour = jnp.zeros((batches, ray_total, feature_count), jnp.float32).at[batch_of, slot_ray].add(colour, mode="drop")
        own_through = 1.0 - jnp.zeros((batches, ray_total), jnp.float32).at[batch_of, slot_ray].add(1.0 - through, mode="drop")
        return own_colour, own_through

    own_colour, own_through = lax.map(forward_region, jnp.arange(regions, dtype=jnp.int32))
    identity = (jnp.zeros((batches, ray_total, feature_count), jnp.float32), jnp.ones((batches, ray_total), jnp.float32))

    def rise(running, element):
        return join_pairs(running, element, descending), running

    def fall(running, element):
        return join_pairs(element, running, descending), running

    total, low_pairs = lax.scan(rise, identity, (own_colour, own_through))
    remainder, high_pairs = lax.scan(fall, identity, (own_colour, own_through), reverse=True)
    pixels = total[0]
    grad_pixel = pixels - target
    near_through = jnp.where(descending[None, :, :, 0], high_pairs[1], low_pairs[1])
    far_colour = jnp.where(descending[None], low_pairs[0], high_pairs[0])
    d_colour_ray = near_through[..., None] * grad_pixel[None]
    d_through_ray = near_through * jnp.sum(grad_pixel[None] * far_colour, axis=-1)

    def backward_region(region):
        batch_of, ray_number, occupied, ray_index, geometry, offsets = region_inputs(region, block_rays, block_offsets, ray_frames, kept_slots)
        weights_here = params_of(region)
        colour, through, stored = block_forward(geometry, offsets, *weights_here)
        d_colour = d_colour_ray[region][batch_of, ray_index] * occupied[:, None]
        d_through = d_through_ray[region][batch_of, ray_index] * occupied
        return block_backward(stored, d_colour, d_through, weights_here[3], weights_here[5], weights_here[6])

    gradients = lax.map(backward_region, jnp.arange(regions, dtype=jnp.int32))
    return (pixels, gradients[0], gradients[1], gradients[2], gradients[3], gradients[4], gradients[5])
```

```python
import functools
import math

import jax
import jax.numpy as jnp
from jax import lax
from jax.experimental import pallas as pl
from jax.experimental.pallas import tpu as pltpu
from jax.sharding import PartitionSpec as P

BLK = 128
CAP = 32
RAYS = 128
FEAT = 64
HID = 256
ENC = 128
REGIONS = 16
BATCHES = 32
CHUNK = 4
ROWS = CHUNK * BLK
STEP = 1.0 / 64.0
F32 = jnp.float32
BF16 = jnp.bfloat16
HIGH = lax.Precision.HIGHEST

TURN_HIGH = 6.28125
TURN_LOW = 2.0 * math.pi - 6.28125
SINE = (
    0.999999994451582,
    -0.16666664569587258,
    0.008333310299565085,
    -0.00019840151845895466,
    2.752938860313289e-06,
    -2.4676381628551014e-08,
    1.3449464950123382e-10,
)


def nn(a, b):
    return lax.dot_general(a, b, (((1,), (0,)), ((), ())), preferred_element_type=F32)


def nt(a, b, precision=None):
    return lax.dot_general(
        a, b, (((1,), (1,)), ((), ())), preferred_element_type=F32, precision=precision
    )


def tn(a, b):
    return lax.dot_general(a, b, (((0,), (0,)), ((), ())), preferred_element_type=F32)


def sine_of(angle, shift):
    turns = jnp.floor(angle * (0.5 / math.pi) + (shift + 0.5))
    rest = (angle - turns * TURN_HIGH) - turns * TURN_LOW + shift * (2.0 * math.pi)
    square = rest * rest
    value = jnp.full_like(rest, SINE[-1])
    for coefficient in SINE[-2::-1]:
        value = value * square + coefficient
    return value * rest


def forward_kernel(
    rays,
    offsets,
    frames,
    freq,
    w_in,
    b_in,
    w_mid,
    b_mid,
    w_heads,
    payload,
    encoded,
    hidden_one,
    hidden_two,
    kept,
    anchor,
    slope,
    heads,
    dens,
):
    lane = lax.broadcasted_iota(jnp.int32, (BLK, 128), 1)
    columns = jnp.concatenate([frames[...], jnp.zeros((2, RAYS), F32)], axis=0).T
    both = jnp.concatenate([freq[...], freq[...]], axis=1)
    anchor[...] = (
        columns[:, 0:1] * both[0:1] + columns[:, 1:2] * both[1:2] + columns[:, 2:3] * both[2:3]
    )
    slope[...] = (
        columns[:, 3:4] * both[0:1] + columns[:, 4:5] * both[1:2] + columns[:, 5:6] * both[2:3]
    )
    dens[...] = jnp.zeros_like(dens)

    rows = lax.broadcasted_iota(jnp.int32, (24, 128), 0)
    cols = lax.broadcasted_iota(jnp.int32, (24, 128), 1)
    low_half = cols < FEAT
    shift = jnp.where(low_half, 0.0, 0.25).astype(F32)
    coarse = rows < 16
    coarse_steps = jnp.where(coarse, 8 * rows, rows - 16).astype(F32)
    sign = jnp.where(low_half[:16], 1.0, -1.0).astype(F32)

    def encode(slot):
        ray = jnp.maximum(rays[slot], 0)
        start = offsets[slot].astype(F32) + 0.5
        base = anchor[pl.ds(ray, 1), :]
        direction = slope[pl.ds(ray, 1), :]
        times = (coarse_steps + jnp.where(coarse, start, 0.0)) * STEP
        angle = jnp.where(coarse, base, 0.0) + times * direction
        table = sine_of(angle, shift)
        swapped = pltpu.roll(table, 64, 1)
        sine_cosine = table[:16]
        quarter_on = swapped[:16] * sign
        fine, fine_swapped = table[16:], swapped[16:]
        fine_sine = jnp.where(low_half[:8], fine, fine_swapped)
        fine_cosine = jnp.where(low_half[:8], fine_swapped, fine)
        parts = [
            sine_cosine[i : i + 1] * fine_cosine + quarter_on[i : i + 1] * fine_sine
            for i in range(16)
        ]
        return jnp.concatenate(parts, axis=0).astype(BF16)

    def chunk(step, carry):
        start = pl.multiple_of(step * ROWS, ROWS)
        enc = jnp.concatenate([encode(step * CHUNK + q) for q in range(CHUNK)], axis=0)
        encoded[pl.ds(start, ROWS), :] = enc
        one = jnp.maximum(nn(enc, w_in[...]) + b_in[...], 0.0).astype(BF16)
        hidden_one[pl.ds(start, ROWS), :] = one
        two = jnp.maximum(nn(one, w_mid[...]) + b_mid[...], 0.0).astype(BF16)
        hidden_two[pl.ds(start, ROWS), :] = two
        both_heads = nn(two, w_heads[...])
        heads[pl.ds(start, ROWS), :] = both_heads
        taken = dens[...]
        for q in range(CHUNK):
            taken = jnp.where(
                lane == FEAT + step * CHUNK + q, both_heads[q * BLK : (q + 1) * BLK], taken
            )
        dens[...] = taken
        return carry

    lax.fori_loop(0, CAP // CHUNK, chunk, 0)

    pre = pltpu.roll(dens[...], 64, 1)
    tau = (jnp.maximum(pre, 0.0) + jnp.log1p(jnp.exp(-jnp.abs(pre)))) * STEP
    row_index = lax.broadcasted_iota(jnp.int32, (BLK, BLK), 0)
    earlier = (lane < row_index).astype(F32)
    before = lax.dot_general(
        earlier, tau, (((1,), (0,)), ((), ())), preferred_element_type=F32, precision=HIGH
    )
    series = tau * (1.0 - tau * (0.5 - tau * (1.0 / 6.0 - tau * (1.0 / 24.0))))
    opacity = jnp.where(tau < 0.03, series, 1.0 - jnp.exp(-tau))
    weight = jnp.exp(-before) * opacity
    passed = jnp.exp(-(before + tau))
    kept[0] = weight
    kept[1] = passed
    kept[2] = jax.nn.sigmoid(pre) * STEP
    last = 1.0 - passed[BLK - 1 : BLK, :]
    lane_row = lane[0:1]
    for slot in range(CAP):
        colour = jnp.sum(
            weight[:, slot : slot + 1] * heads[slot * BLK : (slot + 1) * BLK, :],
            axis=0,
            keepdims=True,
        )
        row = jnp.where(lane_row < FEAT, colour, last[:, slot : slot + 1])
        row = jnp.where(lane_row == 127, rays[slot].astype(F32), row)
        payload[slot : slot + 1, :] = row


def backward_kernel(
    rays,
    place,
    order,
    gathered,
    target,
    w_heads,
    w_mid,
    encoded,
    hidden_one,
    hidden_two,
    kept,
    pixels,
    packed,
    chosen,
    aim,
    slopes,
    proj,
    pre_grad,
    sum_feat,
    sum_mid,
    sum_in,
    bias_mid,
    bias_in,
):
    region = place[0]
    descending = order[0] == 1
    lane = lax.broadcasted_iota(jnp.int32, (BLK, 128), 1)

    own = gathered[region]
    wanted = jnp.concatenate(
        [
            own[:, 127:128],
            (lax.broadcasted_iota(jnp.int32, (8, 1), 0) + 8 * region).astype(F32),
        ],
        axis=0,
    )
    picker = (lax.broadcasted_iota(jnp.int32, (8, 128), 1) == 127).astype(F32)
    group_of = lax.broadcasted_iota(jnp.int32, (40, 128), 1) // CAP
    for group in range(4):
        rows = gathered[4 * group : 4 * group + 4].reshape(128, 128)
        names = nt(picker, rows, HIGH)[0:1]
        same = wanted == names
        left = jnp.concatenate(
            [
                jnp.where(same & (group_of == k), 1.0, 0.0).astype(BF16)
                for k in range(4)
            ],
            axis=0,
        )
        first = rows.astype(BF16)
        rest = rows - first.astype(F32)
        second = rest.astype(BF16)
        third = (rest - second.astype(F32)).astype(BF16)
        found = (nn(left, third) + nn(left, second)) + nn(left, first)
        chosen[4 * group : 4 * group + 4] = found.reshape(4, 40, 128)

    position = jnp.where(descending, REGIONS - 1 - region, region)
    total = jnp.zeros((40, 128), F32)
    through = jnp.ones((40, 128), F32)
    near = jnp.ones((40, 128), F32)
    far = jnp.zeros((40, 128), F32)
    far_through = jnp.ones((40, 128), F32)
    for step in range(REGIONS):
        source = jnp.where(descending, REGIONS - 1 - step, step)
        here = chosen[source]
        through_here = 1.0 - jnp.broadcast_to(here[:, FEAT : FEAT + 1], (40, 128))
        total = total + through * here
        near = jnp.where(step < position, near * through_here, near)
        beyond = step > position
        far = jnp.where(beyond, far + far_through * here, far)
        far_through = jnp.where(beyond, far_through * through_here, far_through)
        through = through * through_here
    pixels[...] = total[32:40, :FEAT]

    for slot in range(CAP):
        slopes[slot : slot + 1, :FEAT] = target[pl.ds(jnp.maximum(rays[slot], 0), 1), :]
    occupied = (own[:, 127:128] >= 0.0) & (lane[:CAP] < FEAT)
    scaled = jnp.where(occupied, near[:CAP] * (total[:CAP] - slopes[...]), 0.0)
    inner = jnp.where(occupied, scaled * far[:CAP], 0.0)
    slopes[...] = scaled
    blank = jnp.zeros((96, 128), F32)
    d_through = nt(jnp.ones((8, 128), F32), jnp.concatenate([inner, blank], axis=0), HIGH)[0:1]
    twice = jnp.concatenate([scaled, scaled, blank[:64]], axis=0)
    direction = nt(w_heads[...].astype(F32), twice, HIGH)
    upper = direction.astype(BF16)
    lower = (direction - upper.astype(F32)).astype(BF16)
    lane_hid = lax.broadcasted_iota(jnp.int32, (HID, 128), 1)
    aim[...] = jnp.where(lane_hid < CAP, upper.astype(F32), lower.astype(F32)).astype(BF16)

    proj[...] = jnp.zeros_like(proj)
    slot_lane = jnp.where(lane < 2 * CAP, lane & (CAP - 1), -1)

    def project(step, carry):
        start = pl.multiple_of(step * ROWS, ROWS)
        part = nn(hidden_two[pl.ds(start, ROWS), :], aim[...])
        taken = proj[...]
        for q in range(CHUNK):
            taken = jnp.where(
                slot_lane == step * CHUNK + q, part[q * BLK : (q + 1) * BLK], taken
            )
        proj[...] = taken
        return carry

    lax.fori_loop(0, CAP // CHUNK, project, 0)
    projected = proj[...] + pltpu.roll(proj[...], 96, 1)
    row_index = lax.broadcasted_iota(jnp.int32, (BLK, BLK), 0)
    later = (lane > row_index).astype(F32)
    weight, passed = kept[0], kept[1]
    behind = lax.dot_general(
        later,
        projected * weight,
        (((1,), (0,)), ((), ())),
        preferred_element_type=F32,
        precision=HIGH,
    )
    d_tau = projected * passed - behind - d_through * passed[BLK - 1 : BLK, :]
    pre_grad[...] = d_tau * kept[2]

    for ref in (sum_feat, sum_mid, sum_in, bias_mid, bias_in):
        ref[...] = jnp.zeros_like(ref)

    def chunk(step, carry):
        start = pl.multiple_of(step * ROWS, ROWS)
        turn = lax.rem(128 - step * CHUNK, 128)
        weights = pltpu.roll(kept[0], turn, 1)
        pres = pltpu.roll(pre_grad[...], turn, 1)
        parts = []
        for q in range(CHUNK):
            colour = slopes[pl.ds(step * CHUNK + q, 1), :]
            pre_here = jnp.where(lane == FEAT, pres[:, q : q + 1], 0.0)
            parts.append(jnp.where(lane < FEAT, weights[:, q : q + 1] * colour, pre_here))
        d_heads = jnp.concatenate(parts, axis=0).astype(BF16)
        two = hidden_two[pl.ds(start, ROWS), :]
        one = hidden_one[pl.ds(start, ROWS), :]
        enc = encoded[pl.ds(start, ROWS), :]
        sum_feat[...] += tn(two, d_heads)
        d_two = jnp.where(two.astype(F32) > 0.0, nt(d_heads, w_heads[...]), 0.0)
        bias_mid[...] += jnp.sum(d_two.reshape(ROWS // 8, 8, HID), axis=0)
        d_two = d_two.astype(BF16)
        sum_mid[...] += tn(one, d_two)
        d_one = jnp.where(one.astype(F32) > 0.0, nt(d_two, w_mid[...]), 0.0)
        bias_in[...] += jnp.sum(d_one.reshape(ROWS // 8, 8, HID), axis=0)
        sum_in[...] += tn(enc, d_one.astype(BF16))
        return carry

    lax.fori_loop(0, CAP // CHUNK, chunk, 0)

    spread = jnp.concatenate(
        [
            jnp.zeros((96, HID), F32),
            jnp.broadcast_to(jnp.sum(bias_in[...], axis=0, keepdims=True), (8, HID)),
            jnp.broadcast_to(jnp.sum(bias_mid[...], axis=0, keepdims=True), (24, HID)),
        ],
        axis=0,
    ).T
    sum_feat[...] = jnp.where(lane_hid < 96, sum_feat[...], spread)
    for part in range(BATCHES):
        packed[part, 0:8, :] = sum_mid[8 * part : 8 * part + 8, 0:128]
        packed[part, 8:16, :] = sum_mid[8 * part : 8 * part + 8, 128:256]
        packed[part, 16:20, :] = sum_in[4 * part : 4 * part + 4, 0:128]
        packed[part, 20:24, :] = sum_in[4 * part : 4 * part + 4, 128:256]
        packed[part, 24:32, :] = sum_feat[8 * part : 8 * part + 8, :]


def finish_kernel(parts, g_in, gb_in, g_mid, gb_mid, g_feat, g_dens):
    total = jnp.sum(parts[...], axis=0)
    g_mid[:, 0:128] = total[0:8]
    g_mid[:, 128:256] = total[8:16]
    g_in[:, 0:128] = total[16:20]
    g_in[:, 128:256] = total[20:24]
    g_feat[...] = total[24:32, :FEAT]
    turned = jnp.concatenate([total[24:32], jnp.zeros((120, 128), F32)], axis=0).T
    g_dens[...] = turned[FEAT : FEAT + 1, 0:8]
    gb_in[...] = turned[96:97, 0:8]
    gb_mid[...] = turned[104:105, 0:8]


VMEM = pl.BlockSpec(memory_space=pltpu.VMEM)
SMEM = pl.BlockSpec(memory_space=pltpu.SMEM)


def shards(
    block_rays,
    block_offsets,
    view_order,
    ray_frames,
    target,
    enc_freq,
    w_in,
    b_in,
    w_mid,
    b_mid,
    w_feat,
    w_dens,
):
    samples = CAP * BLK
    slot_rays = block_rays.reshape(CAP)
    slot_offsets = block_offsets.reshape(CAP)
    w_heads = jnp.concatenate(
        [w_feat[0], jnp.broadcast_to(w_dens[0][:, None], (HID, 128 - FEAT))], axis=1
    )
    payload, encoded, hidden_one, hidden_two, kept = pl.pallas_call(
        forward_kernel,
        name="forward",
        out_shape=(
            jax.ShapeDtypeStruct((CAP, 128), F32),
            jax.ShapeDtypeStruct((samples, ENC), BF16),
            jax.ShapeDtypeStruct((samples, HID), BF16),
            jax.ShapeDtypeStruct((samples, HID), BF16),
            jax.ShapeDtypeStruct((3, BLK, 128), F32),
        ),
        in_specs=[SMEM, SMEM] + [VMEM] * 7,
        out_specs=(VMEM,) * 5,
        scratch_shapes=[
            pltpu.VMEM((RAYS, 128), F32),
            pltpu.VMEM((RAYS, 128), F32),
            pltpu.VMEM((samples, 128), F32),
            pltpu.VMEM((BLK, 128), F32),
        ],
    )(
        slot_rays,
        slot_offsets,
        ray_frames[0],
        enc_freq[0],
        w_in[0],
        b_in,
        w_mid[0],
        b_mid,
        w_heads,
    )
    gathered = lax.all_to_all(
        jnp.broadcast_to(payload[None], (REGIONS, CAP, 128)), "depth", 0, 0, tiled=True
    )
    place = lax.axis_index("depth").astype(jnp.int32).reshape(1)
    pixels, packed = pl.pallas_call(
        backward_kernel,
        name="backward",
        out_shape=(
            jax.ShapeDtypeStruct((8, FEAT), F32),
            jax.ShapeDtypeStruct((BATCHES, 32, 128), F32),
        ),
        in_specs=[SMEM] * 3 + [VMEM] * 8,
        out_specs=(VMEM,) * 2,
        scratch_shapes=[
            pltpu.VMEM((REGIONS, 40, 128), F32),
            pltpu.VMEM((HID, 128), BF16),
            pltpu.VMEM((CAP, 128), F32),
            pltpu.VMEM((BLK, 128), F32),
            pltpu.VMEM((BLK, 128), F32),
            pltpu.VMEM((HID, 128), F32),
            pltpu.VMEM((HID, HID), F32),
            pltpu.VMEM((ENC, HID), F32),
            pltpu.VMEM((8, HID), F32),
            pltpu.VMEM((8, HID), F32),
        ],
    )(
        slot_rays,
        place,
        view_order,
        gathered,
        target[0],
        w_heads,
        w_mid[0],
        encoded,
        hidden_one,
        hidden_two,
        kept,
    )
    received = lax.all_to_all(packed, "cam", 0, 0, tiled=True)
    g_in, gb_in, g_mid, gb_mid, g_feat, g_dens = pl.pallas_call(
        finish_kernel,
        name="finish",
        out_shape=(
            jax.ShapeDtypeStruct((4, HID), F32),
            jax.ShapeDtypeStruct((1, 8), F32),
            jax.ShapeDtypeStruct((8, HID), F32),
            jax.ShapeDtypeStruct((1, 8), F32),
            jax.ShapeDtypeStruct((8, FEAT), F32),
            jax.ShapeDtypeStruct((1, 8), F32),
        ),
        in_specs=[VMEM],
        out_specs=(VMEM,) * 6,
    )(received)
    return (pixels[None], g_in[None], gb_in, g_mid[None], gb_mid, g_feat[None], g_dens)


def solution(mesh):
    placed = (
        P("depth", "cam", None),
        P("depth", "cam", None),
        P("cam"),
        P("cam", None, None),
        P("cam", None, None),
        P("depth", None, None),
        P("depth", None, None),
        P("depth", None),
        P("depth", None, None),
        P("depth", None),
        P("depth", None, None),
        P("depth", None),
    )
    return jax.shard_map(
        shards,
        mesh=mesh,
        in_specs=placed,
        out_specs=(
            P("cam", "depth", None),
            P("depth", "cam", None),
            P("depth", "cam"),
            P("depth", "cam", None),
            P("depth", "cam"),
            P("depth", "cam", None),
            P("depth", "cam"),
        ),
        check_vma=False,
    )
```

```python
import functools
import math

import jax
import jax.numpy as jnp
from jax import lax
from jax.experimental import pallas as pl
from jax.experimental.pallas import tpu as pltpu
from jax.sharding import PartitionSpec as P

BLK = 128
CAP = 32
RAYS = 128
FEAT = 64
HID = 256
ENC = 128
REGIONS = 16
BATCHES = 32
CHUNK = 4
ROWS = CHUNK * BLK
STEP = 1.0 / 64.0
F32 = jnp.float32
BF16 = jnp.bfloat16
HIGH = lax.Precision.HIGHEST

TURN_HIGH = 6.28125
TURN_LOW = 2.0 * math.pi - 6.28125
SINE = (
    0.999999994451582,
    -0.16666664569587258,
    0.008333310299565085,
    -0.00019840151845895466,
    2.752938860313289e-06,
    -2.4676381628551014e-08,
    1.3449464950123382e-10,
)


def nn(a, b):
    return lax.dot_general(a, b, (((1,), (0,)), ((), ())), preferred_element_type=F32)


def nt(a, b, precision=None):
    return lax.dot_general(
        a, b, (((1,), (1,)), ((), ())), preferred_element_type=F32, precision=precision
    )


def tn(a, b):
    return lax.dot_general(a, b, (((0,), (0,)), ((), ())), preferred_element_type=F32)


def thirds(a):
    first = a.astype(BF16)
    rest = a - first.astype(F32)
    second = rest.astype(BF16)
    return first, second, (rest - second.astype(F32)).astype(BF16)


def sine_of(angle, shift):
    turns = jnp.floor(angle * (0.5 / math.pi) + (shift + 0.5))
    rest = (angle - turns * TURN_HIGH) - turns * TURN_LOW + shift * (2.0 * math.pi)
    square = rest * rest
    value = jnp.full_like(rest, SINE[-1])
    for coefficient in SINE[-2::-1]:
        value = value * square + coefficient
    return value * rest


def forward_kernel(
    rays,
    offsets,
    frames_far,
    freq_far,
    w_in_far,
    b_in_far,
    w_mid_far,
    b_mid_far,
    w_feat_far,
    w_dens_far,
    payload,
    encoded_far,
    hidden_one_far,
    hidden_two_far,
    kept_far,
    frames,
    freq,
    w_in,
    b_in,
    w_mid,
    b_mid,
    w_heads,
    w_dens,
    encoded,
    hidden_one,
    hidden_two,
    kept,
    anchor,
    slope,
    heads,
    dens,
    sent,
    in_sems,
    out_sems,
    last_sems,
):
    wanted = (
        (frames_far, frames),
        (freq_far, freq),
        (w_feat_far, w_heads.at[0:FEAT]),
        (w_dens_far, w_dens),
        (w_in_far, w_in),
        (b_in_far, b_in),
        (w_mid_far, w_mid),
        (b_mid_far, b_mid),
    )
    arriving = [
        pltpu.make_async_copy(far, near, in_sems.at[i]) for i, (far, near) in enumerate(wanted)
    ]
    for copy in arriving:
        copy.start()
    for copy in arriving[:2]:
        copy.wait()
    lane = lax.broadcasted_iota(jnp.int32, (BLK, 128), 1)
    columns = jnp.concatenate(
        [frames[c] for c in range(6)] + [jnp.zeros((2, RAYS), F32)], axis=0
    ).T
    both = jnp.concatenate([freq[c] for c in range(3)], axis=0)
    both = jnp.concatenate([both, both], axis=1)
    for copy in arriving[2:]:
        copy.wait()
    w_heads[FEAT:128, :] = jnp.broadcast_to(w_dens[...].astype(F32), (128 - FEAT, HID)).astype(BF16)
    anchor[...] = (
        columns[:, 0:1] * both[0:1] + columns[:, 1:2] * both[1:2] + columns[:, 2:3] * both[2:3]
    )
    slope[...] = (
        columns[:, 3:4] * both[0:1] + columns[:, 4:5] * both[1:2] + columns[:, 5:6] * both[2:3]
    )
    dens[...] = jnp.zeros_like(dens)

    rows = lax.broadcasted_iota(jnp.int32, (24, 128), 0)
    cols = lax.broadcasted_iota(jnp.int32, (24, 128), 1)
    low_half = cols < FEAT
    shift = jnp.where(low_half, 0.0, 0.25).astype(F32)
    coarse = rows < 16
    coarse_steps = jnp.where(coarse, 8 * rows, rows - 16).astype(F32)
    sign = jnp.where(low_half[:16], 1.0, -1.0).astype(F32)

    def encode(slot):
        ray = jnp.maximum(rays[slot], 0)
        start = offsets[slot].astype(F32) + 0.5
        base = anchor[pl.ds(ray, 1), :]
        direction = slope[pl.ds(ray, 1), :]
        times = (coarse_steps + jnp.where(coarse, start, 0.0)) * STEP
        angle = jnp.where(coarse, base, 0.0) + times * direction
        table = sine_of(angle, shift)
        swapped = pltpu.roll(table, 64, 1)
        sine_cosine = table[:16]
        quarter_on = swapped[:16] * sign
        fine, fine_swapped = table[16:], swapped[16:]
        fine_sine = jnp.where(low_half[:8], fine, fine_swapped)
        fine_cosine = jnp.where(low_half[:8], fine_swapped, fine)
        parts = [
            sine_cosine[i : i + 1] * fine_cosine + quarter_on[i : i + 1] * fine_sine
            for i in range(16)
        ]
        return jnp.concatenate(parts, axis=0).astype(BF16)

    def leaving(step):
        span = pl.ds(pl.multiple_of(step * ROWS, ROWS), ROWS)
        pairs = (
            (encoded, encoded_far),
            (hidden_one, hidden_one_far),
            (hidden_two, hidden_two_far),
        )
        return [
            pltpu.make_async_copy(near.at[span], far.at[span], out_sems.at[step, i])
            for i, (near, far) in enumerate(pairs)
        ]

    def chunk(step, carry):
        start = pl.multiple_of(step * ROWS, ROWS)
        enc = jnp.concatenate([encode(step * CHUNK + q) for q in range(CHUNK)], axis=0)
        encoded[pl.ds(start, ROWS), :] = enc
        one = jnp.maximum(nn(enc, w_in[...]) + b_in[...], 0.0).astype(BF16)
        hidden_one[pl.ds(start, ROWS), :] = one
        two = jnp.maximum(nn(one, w_mid[...]) + b_mid[...], 0.0).astype(BF16)
        hidden_two[pl.ds(start, ROWS), :] = two
        both_heads = nt(two, w_heads[...])
        heads[pl.ds(start, ROWS), :] = both_heads
        taken = dens[...]
        for q in range(CHUNK):
            taken = jnp.where(
                lane == FEAT + step * CHUNK + q, both_heads[q * BLK : (q + 1) * BLK], taken
            )
        dens[...] = taken
        for copy in leaving(step):
            copy.start()
        return carry

    lax.fori_loop(0, CAP // CHUNK, chunk, 0)

    pre = pltpu.roll(dens[...], 64, 1)
    tau = (jnp.maximum(pre, 0.0) + jnp.log1p(jnp.exp(-jnp.abs(pre)))) * STEP
    row_index = lax.broadcasted_iota(jnp.int32, (BLK, BLK), 0)
    earlier = (lane < row_index).astype(F32)
    before = lax.dot_general(
        earlier, tau, (((1,), (0,)), ((), ())), preferred_element_type=F32, precision=HIGH
    )
    series = tau * (1.0 - tau * (0.5 - tau * (1.0 / 6.0 - tau * (1.0 / 24.0))))
    opacity = jnp.where(tau < 0.03, series, 1.0 - jnp.exp(-tau))
    weight = jnp.exp(-before) * opacity
    passed = jnp.exp(-(before + tau))
    kept[0] = weight
    kept[1] = passed
    kept[2] = jax.nn.sigmoid(pre) * STEP
    closing = [pltpu.make_async_copy(kept, kept_far, last_sems.at[REGIONS])]
    closing[0].start()
    last = 1.0 - passed[BLK - 1 : BLK, :]
    lane_row = lane[0:1]
    for slot in range(CAP):
        colour = jnp.sum(
            weight[:, slot : slot + 1] * heads[slot * BLK : (slot + 1) * BLK, :],
            axis=0,
            keepdims=True,
        )
        row = jnp.where(lane_row < FEAT, colour, last[:, slot : slot + 1])
        row = jnp.where(lane_row == 127, rays[slot].astype(F32), row)
        sent[slot : slot + 1, :] = row
    for peer in range(REGIONS):
        closing.append(pltpu.make_async_copy(sent, payload.at[peer], last_sems.at[peer]))
        closing[-1].start()
    for step in range(CAP // CHUNK):
        for copy in leaving(step):
            copy.wait()
    for copy in closing:
        copy.wait()


def backward_kernel(
    place,
    order,
    gathered,
    target_far,
    w_feat_far,
    w_dens_far,
    w_mid_far,
    encoded_far,
    hidden_one_far,
    hidden_two_far,
    kept_far,
    pixels,
    packed,
    target,
    w_heads,
    w_dens,
    w_mid,
    encoded,
    hidden_one,
    hidden_two,
    kept,
    chosen,
    aim,
    slopes,
    proj,
    pre_grad,
    sum_feat,
    sum_mid,
    sum_in,
    bias_mid,
    bias_in,
    in_sems,
):
    wanted = (
        (target_far, target),
        (w_feat_far, w_heads.at[0:FEAT]),
        (w_dens_far, w_dens),
        (hidden_two_far, hidden_two),
        (kept_far, kept),
        (hidden_one_far, hidden_one),
        (encoded_far, encoded),
        (w_mid_far, w_mid),
    )
    arriving = [
        pltpu.make_async_copy(far, near, in_sems.at[i]) for i, (far, near) in enumerate(wanted)
    ]
    for copy in arriving:
        copy.start()
    region = place[0]
    descending = order[0] == 1
    lane = lax.broadcasted_iota(jnp.int32, (BLK, 128), 1)

    own = gathered[region]
    wanted = jnp.concatenate(
        [
            own[:, 127:128],
            (lax.broadcasted_iota(jnp.int32, (8, 1), 0) + 8 * region).astype(F32),
        ],
        axis=0,
    )
    picker = (lax.broadcasted_iota(jnp.int32, (8, 128), 1) == 127).astype(F32)
    group_of = lax.broadcasted_iota(jnp.int32, (40, 128), 1) // CAP
    for group in range(4):
        rows = gathered[4 * group : 4 * group + 4].reshape(128, 128)
        names = nt(picker, rows, HIGH)[0:1]
        same = wanted == names
        left = jnp.concatenate(
            [
                jnp.where(same & (group_of == k), 1.0, 0.0).astype(BF16)
                for k in range(4)
            ],
            axis=0,
        )
        first, second, third = thirds(rows)
        found = (nn(left, third) + nn(left, second)) + nn(left, first)
        chosen[4 * group : 4 * group + 4] = found.reshape(4, 40, 128)

    position = jnp.where(descending, REGIONS - 1 - region, region)
    total = jnp.zeros((40, 128), F32)
    through = jnp.ones((40, 128), F32)
    near = jnp.ones((40, 128), F32)
    far = jnp.zeros((40, 128), F32)
    far_through = jnp.ones((40, 128), F32)
    for step in range(REGIONS):
        source = jnp.where(descending, REGIONS - 1 - step, step)
        here = chosen[source]
        through_here = 1.0 - jnp.broadcast_to(here[:, FEAT : FEAT + 1], (40, 128))
        total = total + through * here
        near = jnp.where(step < position, near * through_here, near)
        beyond = step > position
        far = jnp.where(beyond, far + far_through * here, far)
        far_through = jnp.where(beyond, far_through * through_here, far_through)
        through = through * through_here
    pixels[...] = total[32:40, :FEAT]

    for copy in arriving[:3]:
        copy.wait()
    w_heads[FEAT:128, :] = jnp.broadcast_to(w_dens[...].astype(F32), (128 - FEAT, HID)).astype(BF16)
    picked = jnp.where(own[:, 127:128] == lane[:CAP].astype(F32), 1.0, 0.0).astype(BF16)
    first, second, third = thirds(target[...])
    wished = (nt(picked, third) + nt(picked, second)) + nt(picked, first)
    wished = jnp.concatenate([wished, jnp.zeros((CAP, 128 - FEAT), F32)], axis=1)
    occupied = (own[:, 127:128] >= 0.0) & (lane[:CAP] < FEAT)
    scaled = jnp.where(occupied, near[:CAP] * (total[:CAP] - wished), 0.0)
    inner = jnp.where(occupied, scaled * far[:CAP], 0.0)
    slopes[...] = scaled
    blank = jnp.zeros((96, 128), F32)
    d_through = nt(jnp.ones((8, 128), F32), jnp.concatenate([inner, blank], axis=0), HIGH)[0:1]
    twice = jnp.concatenate([scaled, scaled, blank[:64]], axis=0)
    direction = lax.dot_general(
        twice,
        w_heads[...].astype(F32),
        (((1,), (0,)), ((), ())),
        preferred_element_type=F32,
        precision=HIGH,
    )
    upper = direction.astype(BF16)
    lower = (direction - upper.astype(F32)).astype(BF16)
    lane_hid = lax.broadcasted_iota(jnp.int32, (HID, 128), 1)
    slot_row = lax.broadcasted_iota(jnp.int32, (128, HID), 0)
    aim[...] = jnp.where(slot_row < CAP, upper.astype(F32), lower.astype(F32)).astype(BF16)

    proj[...] = jnp.zeros_like(proj)
    slot_lane = jnp.where(lane < 2 * CAP, lane & (CAP - 1), -1)

    def project(step, carry):
        start = pl.multiple_of(step * ROWS, ROWS)
        part = nt(hidden_two[pl.ds(start, ROWS), :], aim[...])
        taken = proj[...]
        for q in range(CHUNK):
            taken = jnp.where(
                slot_lane == step * CHUNK + q, part[q * BLK : (q + 1) * BLK], taken
            )
        proj[...] = taken
        return carry

    for copy in arriving[3:]:
        copy.wait()
    lax.fori_loop(0, CAP // CHUNK, project, 0)
    projected = proj[...] + pltpu.roll(proj[...], 96, 1)
    row_index = lax.broadcasted_iota(jnp.int32, (BLK, BLK), 0)
    later = (lane > row_index).astype(F32)
    weight, passed = kept[0], kept[1]
    behind = lax.dot_general(
        later,
        projected * weight,
        (((1,), (0,)), ((), ())),
        preferred_element_type=F32,
        precision=HIGH,
    )
    d_tau = projected * passed - behind - d_through * passed[BLK - 1 : BLK, :]
    pre_grad[...] = d_tau * kept[2]

    for ref in (sum_feat, sum_mid, sum_in, bias_mid, bias_in):
        ref[...] = jnp.zeros_like(ref)

    def chunk(step, carry):
        start = pl.multiple_of(step * ROWS, ROWS)
        turn = lax.rem(128 - step * CHUNK, 128)
        weights = pltpu.roll(kept[0], turn, 1)
        pres = pltpu.roll(pre_grad[...], turn, 1)
        parts = []
        for q in range(CHUNK):
            colour = slopes[pl.ds(step * CHUNK + q, 1), :]
            pre_here = jnp.where(lane == FEAT, pres[:, q : q + 1], 0.0)
            parts.append(jnp.where(lane < FEAT, weights[:, q : q + 1] * colour, pre_here))
        d_heads = jnp.concatenate(parts, axis=0).astype(BF16)
        two = hidden_two[pl.ds(start, ROWS), :]
        one = hidden_one[pl.ds(start, ROWS), :]
        enc = encoded[pl.ds(start, ROWS), :]
        sum_feat[...] += tn(two, d_heads)
        d_two = jnp.where(two.astype(F32) > 0.0, nn(d_heads, w_heads[...]), 0.0)
        bias_mid[...] += jnp.sum(d_two.reshape(ROWS // 8, 8, HID), axis=0)
        d_two = d_two.astype(BF16)
        sum_mid[...] += tn(one, d_two)
        d_one = jnp.where(one.astype(F32) > 0.0, nt(d_two, w_mid[...]), 0.0)
        bias_in[...] += jnp.sum(d_one.reshape(ROWS // 8, 8, HID), axis=0)
        sum_in[...] += tn(enc, d_one.astype(BF16))
        return carry

    lax.fori_loop(0, CAP // CHUNK, chunk, 0)

    spread = jnp.concatenate(
        [
            jnp.zeros((96, HID), F32),
            jnp.broadcast_to(jnp.sum(bias_in[...], axis=0, keepdims=True), (8, HID)),
            jnp.broadcast_to(jnp.sum(bias_mid[...], axis=0, keepdims=True), (24, HID)),
        ],
        axis=0,
    ).T
    sum_feat[...] = jnp.where(lane_hid < 96, sum_feat[...], spread)
    for part in range(BATCHES):
        packed[part, 0:8, :] = sum_mid[8 * part : 8 * part + 8, 0:128]
        packed[part, 8:16, :] = sum_mid[8 * part : 8 * part + 8, 128:256]
        packed[part, 16:20, :] = sum_in[4 * part : 4 * part + 4, 0:128]
        packed[part, 20:24, :] = sum_in[4 * part : 4 * part + 4, 128:256]
        packed[part, 24:32, :] = sum_feat[8 * part : 8 * part + 8, :]


def finish_kernel(parts, g_in, gb_in, g_mid, gb_mid, g_feat, g_dens):
    total = jnp.sum(parts[...], axis=0)
    g_mid[:, 0:128] = total[0:8]
    g_mid[:, 128:256] = total[8:16]
    g_in[:, 0:128] = total[16:20]
    g_in[:, 128:256] = total[20:24]
    g_feat[...] = total[24:32, :FEAT]
    turned = jnp.concatenate([total[24:32], jnp.zeros((120, 128), F32)], axis=0).T
    g_dens[...] = turned[FEAT : FEAT + 1, 0:8]
    gb_in[...] = turned[96:97, 0:8]
    gb_mid[...] = turned[104:105, 0:8]


VMEM = pl.BlockSpec(memory_space=pltpu.VMEM)
SMEM = pl.BlockSpec(memory_space=pltpu.SMEM)
HBM = pl.BlockSpec(memory_space=pltpu.HBM)
DMA = pltpu.SemaphoreType.DMA


def shards(
    block_rays,
    block_offsets,
    view_order,
    ray_frames,
    target,
    enc_freq,
    w_in,
    b_in,
    w_mid,
    b_mid,
    w_feat,
    w_dens,
):
    samples = CAP * BLK
    slot_rays = block_rays.reshape(CAP)
    slot_offsets = block_offsets.reshape(CAP)
    payload, *stored = pl.pallas_call(
        forward_kernel,
        name="forward",
        out_shape=(
            jax.ShapeDtypeStruct((REGIONS, CAP, 128), F32),
            jax.ShapeDtypeStruct((samples, ENC), BF16),
            jax.ShapeDtypeStruct((samples, HID), BF16),
            jax.ShapeDtypeStruct((samples, HID), BF16),
            jax.ShapeDtypeStruct((3, BLK, 128), F32),
        ),
        in_specs=[SMEM, SMEM] + [HBM] * 8,
        out_specs=(HBM,) * 5,
        scratch_shapes=[
            pltpu.VMEM((6, 1, RAYS), F32),
            pltpu.VMEM((3, 1, FEAT), F32),
            pltpu.VMEM((ENC, HID), BF16),
            pltpu.VMEM((1, HID), F32),
            pltpu.VMEM((HID, HID), BF16),
            pltpu.VMEM((1, HID), F32),
            pltpu.VMEM((128, HID), BF16),
            pltpu.VMEM((1, HID), BF16),
            pltpu.VMEM((samples, ENC), BF16),
            pltpu.VMEM((samples, HID), BF16),
            pltpu.VMEM((samples, HID), BF16),
            pltpu.VMEM((3, BLK, 128), F32),
            pltpu.VMEM((RAYS, 128), F32),
            pltpu.VMEM((RAYS, 128), F32),
            pltpu.VMEM((samples, 128), F32),
            pltpu.VMEM((BLK, 128), F32),
            pltpu.VMEM((CAP, 128), F32),
            DMA((8,)),
            DMA((CAP // CHUNK, 3)),
            DMA((REGIONS + 1,)),
        ],
    )(
        slot_rays,
        slot_offsets,
        ray_frames.transpose(1, 0, 2),
        enc_freq.transpose(1, 0, 2),
        w_in[0],
        b_in,
        w_mid[0],
        b_mid,
        w_feat[0].T,
        w_dens,
    )
    gathered = lax.all_to_all(payload, "depth", 0, 0, tiled=True)
    place = lax.axis_index("depth").astype(jnp.int32).reshape(1)
    pixels, packed = pl.pallas_call(
        backward_kernel,
        name="backward",
        out_shape=(
            jax.ShapeDtypeStruct((8, FEAT), F32),
            jax.ShapeDtypeStruct((BATCHES, 32, 128), F32),
        ),
        in_specs=[SMEM] * 2 + [VMEM] + [HBM] * 8,
        out_specs=(VMEM,) * 2,
        scratch_shapes=[
            pltpu.VMEM((FEAT, RAYS), F32),
            pltpu.VMEM((128, HID), BF16),
            pltpu.VMEM((1, HID), BF16),
            pltpu.VMEM((HID, HID), BF16),
            pltpu.VMEM((samples, ENC), BF16),
            pltpu.VMEM((samples, HID), BF16),
            pltpu.VMEM((samples, HID), BF16),
            pltpu.VMEM((3, BLK, 128), F32),
            pltpu.VMEM((REGIONS, 40, 128), F32),
            pltpu.VMEM((128, HID), BF16),
            pltpu.VMEM((CAP, 128), F32),
            pltpu.VMEM((BLK, 128), F32),
            pltpu.VMEM((BLK, 128), F32),
            pltpu.VMEM((HID, 128), F32),
            pltpu.VMEM((HID, HID), F32),
            pltpu.VMEM((ENC, HID), F32),
            pltpu.VMEM((8, HID), F32),
            pltpu.VMEM((8, HID), F32),
            DMA((8,)),
        ],
    )(
        place,
        view_order,
        pltpu.with_memory_space_constraint(gathered, pltpu.VMEM),
        target[0].T,
        w_feat[0].T,
        w_dens,
        w_mid[0],
        *stored,
    )
    received = lax.all_to_all(packed, "cam", 0, 0, tiled=True)
    g_in, gb_in, g_mid, gb_mid, g_feat, g_dens = pl.pallas_call(
        finish_kernel,
        name="finish",
        out_shape=(
            jax.ShapeDtypeStruct((4, HID), F32),
            jax.ShapeDtypeStruct((1, 8), F32),
            jax.ShapeDtypeStruct((8, HID), F32),
            jax.ShapeDtypeStruct((1, 8), F32),
            jax.ShapeDtypeStruct((8, FEAT), F32),
            jax.ShapeDtypeStruct((1, 8), F32),
        ),
        in_specs=[VMEM],
        out_specs=(VMEM,) * 6,
    )(received)
    return (pixels[None], g_in[None], gb_in, g_mid[None], gb_mid, g_feat[None], g_dens)


def solution(mesh):
    placed = (
        P("depth", "cam", None),
        P("depth", "cam", None),
        P("cam"),
        P("cam", None, None),
        P("cam", None, None),
        P("depth", None, None),
        P("depth", None, None),
        P("depth", None),
        P("depth", None, None),
        P("depth", None),
        P("depth", None, None),
        P("depth", None),
    )
    return jax.shard_map(
        shards,
        mesh=mesh,
        in_specs=placed,
        out_specs=(
            P("cam", "depth", None),
            P("depth", "cam", None),
            P("depth", "cam"),
            P("depth", "cam", None),
            P("depth", "cam"),
            P("depth", "cam", None),
            P("depth", "cam"),
        ),
        check_vma=False,
    )
```

```python
import functools
import math

import jax
import jax.numpy as jnp
from jax import lax
from jax.experimental import pallas as pl
from jax.experimental.pallas import tpu as pltpu
from jax.sharding import PartitionSpec as P

BLK = 128
CAP = 32
RAYS = 128
FEAT = 64
HID = 256
ENC = 128
REGIONS = 16
BATCHES = 32
FORWARD_CHUNK = 16
BACKWARD_CHUNK = 8
STEP = 1.0 / 64.0
F32 = jnp.float32
BF16 = jnp.bfloat16
HIGH = lax.Precision.HIGHEST

TURN_HIGH = 6.28125
TURN_LOW = 2.0 * math.pi - 6.28125
SINE = (
    0.999999994451582,
    -0.16666664569587258,
    0.008333310299565085,
    -0.00019840151845895466,
    2.752938860313289e-06,
    -2.4676381628551014e-08,
    1.3449464950123382e-10,
)


def nn(a, b):
    return lax.dot_general(a, b, (((1,), (0,)), ((), ())), preferred_element_type=F32)


def nt(a, b, precision=None):
    return lax.dot_general(
        a, b, (((1,), (1,)), ((), ())), preferred_element_type=F32, precision=precision
    )


def tn(a, b):
    return lax.dot_general(a, b, (((0,), (0,)), ((), ())), preferred_element_type=F32)


def thirds(a):
    first = a.astype(BF16)
    rest = a - first.astype(F32)
    second = rest.astype(BF16)
    return first, second, (rest - second.astype(F32)).astype(BF16)


def stacked(a, parts):
    return jnp.concatenate(thirds(a)[:parts], axis=0)


def folded(a, parts):
    rows = a.shape[0] // parts
    total = a[(parts - 1) * rows :]
    for part in range(parts - 2, -1, -1):
        total = total + a[part * rows : (part + 1) * rows]
    return total


def sine_of(angle, shift):
    turns = jnp.floor(angle * (0.5 / math.pi) + (shift + 0.5))
    rest = (angle - turns * TURN_HIGH) - turns * TURN_LOW + shift * (2.0 * math.pi)
    square = rest * rest
    value = jnp.full_like(rest, SINE[-1])
    for coefficient in SINE[-2::-1]:
        value = value * square + coefficient
    return value * rest


def forward_kernel(
    rays,
    offsets,
    frames_far,
    freq_far,
    w_in_far,
    b_in_far,
    w_mid_far,
    b_mid_far,
    w_feat_far,
    w_dens_far,
    payload,
    encoded_far,
    hidden_one_far,
    hidden_two_far,
    kept_far,
    frames,
    freq,
    w_in,
    b_in,
    w_mid,
    b_mid,
    w_heads,
    w_dens,
    encoded,
    hidden_one,
    hidden_two,
    kept,
    anchor,
    slope,
    dens,
    sent,
    in_sems,
    out_sems,
    last_sems,
):
    wanted = (
        (frames_far, frames),
        (freq_far, freq),
        (w_feat_far, w_heads.at[0:FEAT]),
        (w_dens_far, w_dens),
        (w_in_far, w_in),
        (b_in_far, b_in),
        (w_mid_far, w_mid),
        (b_mid_far, b_mid),
    )
    arriving = [
        pltpu.make_async_copy(far, near, in_sems.at[i]) for i, (far, near) in enumerate(wanted)
    ]
    for copy in arriving:
        copy.start()
    for copy in arriving[:2]:
        copy.wait()
    rows_each = FORWARD_CHUNK * BLK
    lane = lax.broadcasted_iota(jnp.int32, (BLK, 128), 1)
    columns = jnp.concatenate(
        [frames[c] for c in range(6)] + [jnp.zeros((2, RAYS), F32)], axis=0
    ).T
    both = jnp.concatenate([freq[c] for c in range(3)], axis=0)
    both = jnp.concatenate([both, both], axis=1)
    for copy in arriving[2:]:
        copy.wait()
    w_heads[FEAT:128, :] = jnp.broadcast_to(w_dens[...].astype(F32), (128 - FEAT, HID)).astype(BF16)
    anchor[...] = (
        columns[:, 0:1] * both[0:1] + columns[:, 1:2] * both[1:2] + columns[:, 2:3] * both[2:3]
    )
    slope[...] = (
        columns[:, 3:4] * both[0:1] + columns[:, 4:5] * both[1:2] + columns[:, 5:6] * both[2:3]
    )
    dens[...] = jnp.zeros_like(dens)

    rows = lax.broadcasted_iota(jnp.int32, (24, 128), 0)
    cols = lax.broadcasted_iota(jnp.int32, (24, 128), 1)
    low_half = cols < FEAT
    shift = jnp.where(low_half, 0.0, 0.25).astype(F32)
    coarse = rows < 16
    coarse_steps = jnp.where(coarse, 8 * rows, rows - 16).astype(F32)
    sign = jnp.where(low_half[:16], 1.0, -1.0).astype(F32)

    def encode(slot):
        ray = jnp.maximum(rays[slot], 0)
        start = offsets[slot].astype(F32) + 0.5
        base = anchor[pl.ds(ray, 1), :]
        direction = slope[pl.ds(ray, 1), :]
        times = (coarse_steps + jnp.where(coarse, start, 0.0)) * STEP
        angle = jnp.where(coarse, base, 0.0) + times * direction
        table = sine_of(angle, shift)
        swapped = pltpu.roll(table, 64, 1)
        sine_cosine = table[:16]
        quarter_on = swapped[:16] * sign
        fine, fine_swapped = table[16:], swapped[16:]
        fine_sine = jnp.where(low_half[:8], fine, fine_swapped)
        fine_cosine = jnp.where(low_half[:8], fine_swapped, fine)
        parts = [
            sine_cosine[i : i + 1] * fine_cosine + quarter_on[i : i + 1] * fine_sine
            for i in range(16)
        ]
        return jnp.concatenate(parts, axis=0).astype(BF16)

    def leaving(step):
        span = pl.ds(pl.multiple_of(step * rows_each, rows_each), rows_each)
        pairs = (
            (encoded, encoded_far),
            (hidden_one, hidden_one_far),
            (hidden_two, hidden_two_far),
        )
        return [
            pltpu.make_async_copy(near.at[span], far.at[span], out_sems.at[step, i])
            for i, (near, far) in enumerate(pairs)
        ]

    def chunk(step, carry):
        start = pl.multiple_of(step * rows_each, rows_each)
        enc = jnp.concatenate([encode(step * FORWARD_CHUNK + q) for q in range(FORWARD_CHUNK)], axis=0)
        encoded[pl.ds(start, rows_each), :] = enc
        one = jnp.maximum(nn(enc, w_in[...]) + b_in[...], 0.0).astype(BF16)
        hidden_one[pl.ds(start, rows_each), :] = one
        two = jnp.maximum(nn(one, w_mid[...]) + b_mid[...], 0.0).astype(BF16)
        hidden_two[pl.ds(start, rows_each), :] = two
        both_heads = nt(two, w_heads[...])
        taken = dens[...]
        for q in range(FORWARD_CHUNK):
            taken = jnp.where(
                lane == FEAT + step * FORWARD_CHUNK + q, both_heads[q * BLK : (q + 1) * BLK], taken
            )
        dens[...] = taken
        for copy in leaving(step):
            copy.start()
        return carry

    lax.fori_loop(0, CAP // FORWARD_CHUNK, chunk, 0)

    pre = dens[...].T[FEAT : FEAT + CAP]
    tau = (jnp.maximum(pre, 0.0) + jnp.log1p(jnp.exp(-jnp.abs(pre)))) * STEP
    row_index = lax.broadcasted_iota(jnp.int32, (BLK, BLK), 0)
    earlier = jnp.where(row_index < lane, 1.0, 0.0).astype(BF16)
    before = folded(nn(stacked(tau, 3), earlier), 3)
    series = tau * (1.0 - tau * (0.5 - tau * (1.0 / 6.0 - tau * (1.0 / 24.0))))
    opacity = jnp.where(tau < 0.03, series, 1.0 - jnp.exp(-tau))
    weight = jnp.exp(-before) * opacity
    passed = jnp.exp(-(before + tau))
    kept[0] = weight
    kept[1] = passed
    kept[2] = jax.nn.sigmoid(pre) * STEP
    closing = [pltpu.make_async_copy(kept, kept_far, last_sems.at[REGIONS])]
    closing[0].start()
    weight_parts = stacked(weight, 2).astype(F32)
    slot_row = lax.broadcasted_iota(jnp.int32, (2 * CAP, 128), 0) & (CAP - 1)
    spread = jnp.concatenate(
        [jnp.where(slot_row == slot, weight_parts, 0.0).astype(BF16) for slot in range(CAP)],
        axis=1,
    )
    blended = folded(nn(spread, hidden_two[...]), 2)
    colour = folded(nt(stacked(blended, 2), w_heads[...]), 2)
    row8 = lax.broadcasted_iota(jnp.int32, (8, 128), 0)
    names = []
    for tile in range(CAP // 8):
        name = jnp.zeros((8, 128), F32)
        for k in range(8):
            name = jnp.where(row8 == k, rays[8 * tile + k].astype(F32), name)
        names.append(name)
    names = jnp.concatenate(names, axis=0)
    lane_row = lane[:CAP]
    row = jnp.where(lane_row < FEAT, colour, 1.0 - passed[:, BLK - 1 : BLK])
    sent[...] = jnp.where(lane_row == 127, names, row)
    for peer in range(REGIONS):
        closing.append(pltpu.make_async_copy(sent, payload.at[peer], last_sems.at[peer]))
        closing[-1].start()
    for step in range(CAP // FORWARD_CHUNK):
        for copy in leaving(step):
            copy.wait()
    for copy in closing:
        copy.wait()


def backward_kernel(
    place,
    order,
    gathered,
    target_far,
    w_feat_far,
    w_dens_far,
    w_mid_far,
    encoded_far,
    hidden_one_far,
    hidden_two_far,
    kept_far,
    pixels,
    packed,
    target,
    w_heads,
    w_dens,
    w_mid,
    encoded,
    hidden_one,
    hidden_two,
    kept,
    chosen,
    aim,
    slopes,
    proj,
    columns,
    sum_feat,
    sum_mid,
    sum_in,
    bias_mid,
    bias_in,
    in_sems,
):
    wanted = (
        (target_far, target),
        (w_feat_far, w_heads.at[0:FEAT]),
        (w_dens_far, w_dens),
        (hidden_two_far, hidden_two),
        (kept_far, kept),
        (hidden_one_far, hidden_one),
        (encoded_far, encoded),
        (w_mid_far, w_mid),
    )
    arriving = [
        pltpu.make_async_copy(far, near, in_sems.at[i]) for i, (far, near) in enumerate(wanted)
    ]
    for copy in arriving:
        copy.start()
    rows_each = BACKWARD_CHUNK * BLK
    region = place[0]
    descending = order[0] == 1
    lane = lax.broadcasted_iota(jnp.int32, (BLK, 128), 1)

    own = gathered[region]
    wanted = jnp.concatenate(
        [
            own[:, 127:128],
            (lax.broadcasted_iota(jnp.int32, (8, 1), 0) + 8 * region).astype(F32),
        ],
        axis=0,
    )
    picker = jnp.where(lane[:16] == 127, 1.0, 0.0).astype(BF16)
    group_of = lax.broadcasted_iota(jnp.int32, (40, 128), 1) // CAP
    for group in range(4):
        rows = gathered[4 * group : 4 * group + 4].reshape(128, 128)
        first, second, third = thirds(rows)
        names = nt(picker, first)[0:1]
        same = wanted == names
        left = jnp.concatenate(
            [jnp.where(same & (group_of == k), 1.0, 0.0).astype(BF16) for k in range(4)],
            axis=0,
        )
        found = (nn(left, third) + nn(left, second)) + nn(left, first)
        chosen[4 * group : 4 * group + 4] = found.reshape(4, 40, 128)

    position = jnp.where(descending, REGIONS - 1 - region, region)
    total = jnp.zeros((40, 128), F32)
    through = jnp.ones((40, 128), F32)
    near = jnp.ones((40, 128), F32)
    far = jnp.zeros((40, 128), F32)
    far_through = jnp.ones((40, 128), F32)
    for step in range(REGIONS):
        source = jnp.where(descending, REGIONS - 1 - step, step)
        here = chosen[source]
        through_here = 1.0 - jnp.broadcast_to(here[:, FEAT : FEAT + 1], (40, 128))
        total = total + through * here
        near = jnp.where(step < position, near * through_here, near)
        beyond = step > position
        far = jnp.where(beyond, far + far_through * here, far)
        far_through = jnp.where(beyond, far_through * through_here, far_through)
        through = through * through_here
    pixels[...] = total[32:40, :FEAT]

    for copy in arriving[:3]:
        copy.wait()
    w_heads[FEAT:128, :] = jnp.broadcast_to(w_dens[...].astype(F32), (128 - FEAT, HID)).astype(BF16)
    picked = jnp.where(own[:, 127:128] == lane[:CAP].astype(F32), 1.0, 0.0).astype(BF16)
    first, second, third = thirds(target[...])
    wished = (nt(picked, third) + nt(picked, second)) + nt(picked, first)
    wished = jnp.concatenate([wished, jnp.zeros((CAP, 128 - FEAT), F32)], axis=1)
    occupied = (own[:, 127:128] >= 0.0) & (lane[:CAP] < FEAT)
    scaled = jnp.where(occupied, near[:CAP] * (total[:CAP] - wished), 0.0)
    inner = jnp.where(occupied, scaled * far[:CAP], 0.0)
    slopes[...] = scaled
    d_through = jnp.sum(inner, axis=1, keepdims=True)
    direction = folded(nn(stacked(scaled, 3), w_heads[...]), 3)
    upper = direction.astype(BF16)
    lower = (direction - upper.astype(F32)).astype(BF16)
    aim[0:CAP, :] = upper
    aim[CAP : 2 * CAP, :] = lower
    aim[2 * CAP : 128, :] = jnp.zeros((128 - 2 * CAP, HID), BF16)

    proj[...] = jnp.zeros_like(proj)
    slot_lane = jnp.where(lane < 2 * CAP, lane & (CAP - 1), -1)

    def project(step, carry):
        start = pl.multiple_of(step * rows_each, rows_each)
        part = nt(hidden_two[pl.ds(start, rows_each), :], aim[...])
        taken = proj[...]
        for q in range(BACKWARD_CHUNK):
            taken = jnp.where(
                slot_lane == step * BACKWARD_CHUNK + q, part[q * BLK : (q + 1) * BLK], taken
            )
        proj[...] = taken
        return carry

    arriving[3].wait()
    lax.fori_loop(0, CAP // BACKWARD_CHUNK, project, 0)
    turned = proj[...].T
    projected = turned[0:CAP] + turned[CAP : 2 * CAP]
    arriving[4].wait()
    row_index = lax.broadcasted_iota(jnp.int32, (BLK, BLK), 0)
    later = jnp.where(row_index > lane, 1.0, 0.0).astype(BF16)
    weight, passed = kept[0], kept[1]
    behind = folded(nn(stacked(projected * weight, 3), later), 3)
    d_tau = projected * passed - behind - d_through * passed[:, BLK - 1 : BLK]
    columns[...] = jnp.concatenate(
        [weight, d_tau * kept[2], jnp.zeros((128 - 2 * CAP, BLK), F32)], axis=0
    ).T
    for copy in arriving[5:]:
        copy.wait()

    for ref in (sum_feat, sum_mid, sum_in, bias_mid, bias_in):
        ref[...] = jnp.zeros_like(ref)

    def chunk(step, carry):
        start = pl.multiple_of(step * rows_each, rows_each)
        turn = lax.rem(128 - step * BACKWARD_CHUNK, 128)
        here = pltpu.roll(columns[...], turn, 1)
        parts = []
        for q in range(BACKWARD_CHUNK):
            colour = slopes[pl.ds(step * BACKWARD_CHUNK + q, 1), :]
            pre_here = jnp.where(lane == FEAT, here[:, CAP + q : CAP + q + 1], 0.0)
            parts.append(jnp.where(lane < FEAT, here[:, q : q + 1] * colour, pre_here))
        d_heads = jnp.concatenate(parts, axis=0).astype(BF16)
        two = hidden_two[pl.ds(start, rows_each), :]
        one = hidden_one[pl.ds(start, rows_each), :]
        enc = encoded[pl.ds(start, rows_each), :]
        sum_feat[...] += tn(two, d_heads)
        d_two = jnp.where(two.astype(F32) > 0.0, nn(d_heads, w_heads[...]), 0.0)
        bias_mid[...] += jnp.sum(d_two.reshape(rows_each // 8, 8, HID), axis=0)
        d_two = d_two.astype(BF16)
        sum_mid[...] += tn(one, d_two)
        d_one = jnp.where(one.astype(F32) > 0.0, nt(d_two, w_mid[...]), 0.0)
        bias_in[...] += jnp.sum(d_one.reshape(rows_each // 8, 8, HID), axis=0)
        sum_in[...] += tn(enc, d_one.astype(BF16))
        return carry

    lax.fori_loop(0, CAP // BACKWARD_CHUNK, chunk, 0)

    spread = jnp.concatenate(
        [
            jnp.zeros((96, HID), F32),
            jnp.broadcast_to(jnp.sum(bias_in[...], axis=0, keepdims=True), (8, HID)),
            jnp.broadcast_to(jnp.sum(bias_mid[...], axis=0, keepdims=True), (24, HID)),
        ],
        axis=0,
    ).T
    sum_feat[...] = jnp.where(lax.broadcasted_iota(jnp.int32, (HID, 128), 1) < 96, sum_feat[...], spread)
    for part in range(BATCHES):
        packed[part, 0:8, :] = sum_mid[8 * part : 8 * part + 8, 0:128]
        packed[part, 8:16, :] = sum_mid[8 * part : 8 * part + 8, 128:256]
        packed[part, 16:20, :] = sum_in[4 * part : 4 * part + 4, 0:128]
        packed[part, 20:24, :] = sum_in[4 * part : 4 * part + 4, 128:256]
        packed[part, 24:32, :] = sum_feat[8 * part : 8 * part + 8, :]


def finish_kernel(parts, g_in, gb_in, g_mid, gb_mid, g_feat, g_dens):
    total = jnp.sum(parts[...], axis=0)
    g_mid[:, 0:128] = total[0:8]
    g_mid[:, 128:256] = total[8:16]
    g_in[:, 0:128] = total[16:20]
    g_in[:, 128:256] = total[20:24]
    g_feat[...] = total[24:32, :FEAT]
    turned = jnp.concatenate([total[24:32], jnp.zeros((120, 128), F32)], axis=0).T
    g_dens[...] = turned[FEAT : FEAT + 1, 0:8]
    gb_in[...] = turned[96:97, 0:8]
    gb_mid[...] = turned[104:105, 0:8]


VMEM = pl.BlockSpec(memory_space=pltpu.VMEM)
SMEM = pl.BlockSpec(memory_space=pltpu.SMEM)
HBM = pl.BlockSpec(memory_space=pltpu.HBM)
DMA = pltpu.SemaphoreType.DMA


def shards(
    block_rays,
    block_offsets,
    view_order,
    ray_frames,
    target,
    enc_freq,
    w_in,
    b_in,
    w_mid,
    b_mid,
    w_feat,
    w_dens,
):
    samples = CAP * BLK
    slot_rays = block_rays.reshape(CAP)
    slot_offsets = block_offsets.reshape(CAP)
    payload, *stored = pl.pallas_call(
        forward_kernel,
        name="forward",
        out_shape=(
            jax.ShapeDtypeStruct((REGIONS, CAP, 128), F32),
            jax.ShapeDtypeStruct((samples, ENC), BF16),
            jax.ShapeDtypeStruct((samples, HID), BF16),
            jax.ShapeDtypeStruct((samples, HID), BF16),
            jax.ShapeDtypeStruct((3, CAP, BLK), F32),
        ),
        in_specs=[SMEM, SMEM] + [HBM] * 8,
        out_specs=(HBM,) * 5,
        scratch_shapes=[
            pltpu.VMEM((6, 1, RAYS), F32),
            pltpu.VMEM((3, 1, FEAT), F32),
            pltpu.VMEM((ENC, HID), BF16),
            pltpu.VMEM((1, HID), F32),
            pltpu.VMEM((HID, HID), BF16),
            pltpu.VMEM((1, HID), F32),
            pltpu.VMEM((128, HID), BF16),
            pltpu.VMEM((1, HID), BF16),
            pltpu.VMEM((samples, ENC), BF16),
            pltpu.VMEM((samples, HID), BF16),
            pltpu.VMEM((samples, HID), BF16),
            pltpu.VMEM((3, CAP, BLK), F32),
            pltpu.VMEM((RAYS, 128), F32),
            pltpu.VMEM((RAYS, 128), F32),
            pltpu.VMEM((BLK, 128), F32),
            pltpu.VMEM((CAP, 128), F32),
            DMA((8,)),
            DMA((CAP // FORWARD_CHUNK, 3)),
            DMA((REGIONS + 1,)),
        ],
    )(
        slot_rays,
        slot_offsets,
        ray_frames.transpose(1, 0, 2),
        enc_freq.transpose(1, 0, 2),
        w_in[0],
        b_in,
        w_mid[0],
        b_mid,
        w_feat[0].T,
        w_dens,
    )
    gathered = lax.all_to_all(payload, "depth", 0, 0, tiled=True)
    place = lax.axis_index("depth").astype(jnp.int32).reshape(1)
    pixels, packed = pl.pallas_call(
        backward_kernel,
        name="backward",
        out_shape=(
            jax.ShapeDtypeStruct((8, FEAT), F32),
            jax.ShapeDtypeStruct((BATCHES, 32, 128), F32),
        ),
        in_specs=[SMEM] * 2 + [VMEM] + [HBM] * 8,
        out_specs=(VMEM,) * 2,
        scratch_shapes=[
            pltpu.VMEM((FEAT, RAYS), F32),
            pltpu.VMEM((128, HID), BF16),
            pltpu.VMEM((1, HID), BF16),
            pltpu.VMEM((HID, HID), BF16),
            pltpu.VMEM((samples, ENC), BF16),
            pltpu.VMEM((samples, HID), BF16),
            pltpu.VMEM((samples, HID), BF16),
            pltpu.VMEM((3, CAP, BLK), F32),
            pltpu.VMEM((REGIONS, 40, 128), F32),
            pltpu.VMEM((128, HID), BF16),
            pltpu.VMEM((CAP, 128), F32),
            pltpu.VMEM((BLK, 128), F32),
            pltpu.VMEM((BLK, 128), F32),
            pltpu.VMEM((HID, 128), F32),
            pltpu.VMEM((HID, HID), F32),
            pltpu.VMEM((ENC, HID), F32),
            pltpu.VMEM((8, HID), F32),
            pltpu.VMEM((8, HID), F32),
            DMA((8,)),
        ],
    )(
        place,
        view_order,
        pltpu.with_memory_space_constraint(gathered, pltpu.VMEM),
        target[0].T,
        w_feat[0].T,
        w_dens,
        w_mid[0],
        *stored,
    )
    received = lax.all_to_all(packed, "cam", 0, 0, tiled=True)
    g_in, gb_in, g_mid, gb_mid, g_feat, g_dens = pl.pallas_call(
        finish_kernel,
        name="finish",
        out_shape=(
            jax.ShapeDtypeStruct((4, HID), F32),
            jax.ShapeDtypeStruct((1, 8), F32),
            jax.ShapeDtypeStruct((8, HID), F32),
            jax.ShapeDtypeStruct((1, 8), F32),
            jax.ShapeDtypeStruct((8, FEAT), F32),
            jax.ShapeDtypeStruct((1, 8), F32),
        ),
        in_specs=[VMEM],
        out_specs=(VMEM,) * 6,
    )(pltpu.with_memory_space_constraint(received, pltpu.VMEM))
    return (pixels[None], g_in[None], gb_in, g_mid[None], gb_mid, g_feat[None], g_dens)


def solution(mesh):
    placed = (
        P("depth", "cam", None),
        P("depth", "cam", None),
        P("cam"),
        P("cam", None, None),
        P("cam", None, None),
        P("depth", None, None),
        P("depth", None, None),
        P("depth", None),
        P("depth", None, None),
        P("depth", None),
        P("depth", None, None),
        P("depth", None),
    )
    return jax.shard_map(
        shards,
        mesh=mesh,
        in_specs=placed,
        out_specs=(
            P("cam", "depth", None),
            P("depth", "cam", None),
            P("depth", "cam"),
            P("depth", "cam", None),
            P("depth", "cam"),
            P("depth", "cam", None),
            P("depth", "cam"),
        ),
        check_vma=False,
    )
```

```python
import functools
import math

import jax
import jax.numpy as jnp
from jax import lax
from jax.experimental import pallas as pl
from jax.experimental.pallas import tpu as pltpu
from jax.sharding import PartitionSpec as P

BLK = 128
CAP = 32
RAYS = 128
FEAT = 64
HID = 256
ENC = 128
REGIONS = 16
BATCHES = 32
FORWARD_CHUNK = 16
BACKWARD_CHUNK = 8
LINES = CAP * FEAT // 128 + 1
STEP = 1.0 / 64.0
F32 = jnp.float32
BF16 = jnp.bfloat16
HIGH = lax.Precision.HIGHEST

TURN_HIGH = 6.28125
TURN_LOW = 2.0 * math.pi - 6.28125
SINE = (
    0.999999994451582,
    -0.16666664569587258,
    0.008333310299565085,
    -0.00019840151845895466,
    2.752938860313289e-06,
    -2.4676381628551014e-08,
    1.3449464950123382e-10,
)


def nn(a, b):
    return lax.dot_general(a, b, (((1,), (0,)), ((), ())), preferred_element_type=F32)


def nt(a, b, precision=None):
    return lax.dot_general(
        a, b, (((1,), (1,)), ((), ())), preferred_element_type=F32, precision=precision
    )


def tn(a, b):
    return lax.dot_general(a, b, (((0,), (0,)), ((), ())), preferred_element_type=F32)


def thirds(a):
    first = a.astype(BF16)
    rest = a - first.astype(F32)
    second = rest.astype(BF16)
    return first, second, (rest - second.astype(F32)).astype(BF16)


def stacked(a, parts):
    return jnp.concatenate(thirds(a)[:parts], axis=0)


def folded(a, parts):
    rows = a.shape[0] // parts
    total = a[(parts - 1) * rows :]
    for part in range(parts - 2, -1, -1):
        total = total + a[part * rows : (part + 1) * rows]
    return total


def sine_of(angle, shift):
    turns = jnp.floor(angle * (0.5 / math.pi) + (shift + 0.5))
    rest = (angle - turns * TURN_HIGH) - turns * TURN_LOW + shift * (2.0 * math.pi)
    square = rest * rest
    value = jnp.full_like(rest, SINE[-1])
    for coefficient in SINE[-2::-1]:
        value = value * square + coefficient
    return value * rest


def forward_kernel(
    rays,
    offsets,
    frames_far,
    freq_far,
    w_in_far,
    b_in_far,
    w_mid_far,
    b_mid_far,
    w_feat_far,
    w_dens_far,
    payload,
    encoded_far,
    hidden_one_far,
    hidden_two_far,
    kept_far,
    frames,
    freq,
    w_in,
    b_in,
    w_mid,
    b_mid,
    w_heads,
    w_dens,
    encoded,
    hidden_one,
    hidden_two,
    kept,
    anchor,
    slope,
    dens,
    sent,
    in_sems,
    out_sems,
    last_sems,
):
    wanted = (
        (frames_far, frames),
        (freq_far, freq),
        (w_feat_far, w_heads.at[0:FEAT]),
        (w_dens_far, w_dens),
        (w_in_far, w_in),
        (b_in_far, b_in),
        (w_mid_far, w_mid),
        (b_mid_far, b_mid),
    )
    arriving = [
        pltpu.make_async_copy(far, near, in_sems.at[i]) for i, (far, near) in enumerate(wanted)
    ]
    for copy in arriving:
        copy.start()
    for copy in arriving[:2]:
        copy.wait()
    rows_each = FORWARD_CHUNK * BLK
    lane = lax.broadcasted_iota(jnp.int32, (BLK, 128), 1)
    columns = jnp.concatenate(
        [frames[c] for c in range(6)] + [jnp.zeros((2, RAYS), F32)], axis=0
    ).T
    both = jnp.concatenate([freq[c] for c in range(3)], axis=0)
    both = jnp.concatenate([both, both], axis=1)
    for copy in arriving[2:]:
        copy.wait()
    w_heads[FEAT:128, :] = jnp.broadcast_to(w_dens[...].astype(F32), (128 - FEAT, HID)).astype(BF16)
    anchor[...] = (
        columns[:, 0:1] * both[0:1] + columns[:, 1:2] * both[1:2] + columns[:, 2:3] * both[2:3]
    )
    slope[...] = (
        columns[:, 3:4] * both[0:1] + columns[:, 4:5] * both[1:2] + columns[:, 5:6] * both[2:3]
    )
    dens[...] = jnp.zeros_like(dens)

    rows = lax.broadcasted_iota(jnp.int32, (24, 128), 0)
    cols = lax.broadcasted_iota(jnp.int32, (24, 128), 1)
    low_half = cols < FEAT
    shift = jnp.where(low_half, 0.0, 0.25).astype(F32)
    coarse = rows < 16
    coarse_steps = jnp.where(coarse, 8 * rows, rows - 16).astype(F32)
    sign = jnp.where(low_half[:16], 1.0, -1.0).astype(F32)

    def encode(slot):
        ray = jnp.maximum(rays[slot], 0)
        start = offsets[slot].astype(F32) + 0.5
        base = anchor[pl.ds(ray, 1), :]
        direction = slope[pl.ds(ray, 1), :]
        times = (coarse_steps + jnp.where(coarse, start, 0.0)) * STEP
        angle = jnp.where(coarse, base, 0.0) + times * direction
        table = sine_of(angle, shift)
        swapped = pltpu.roll(table, 64, 1)
        sine_cosine = table[:16]
        quarter_on = swapped[:16] * sign
        fine, fine_swapped = table[16:], swapped[16:]
        fine_sine = jnp.where(low_half[:8], fine, fine_swapped)
        fine_cosine = jnp.where(low_half[:8], fine_swapped, fine)
        parts = [
            sine_cosine[i : i + 1] * fine_cosine + quarter_on[i : i + 1] * fine_sine
            for i in range(16)
        ]
        return jnp.concatenate(parts, axis=0).astype(BF16)

    def leaving(step):
        span = pl.ds(pl.multiple_of(step * rows_each, rows_each), rows_each)
        pairs = (
            (encoded, encoded_far),
            (hidden_one, hidden_one_far),
            (hidden_two, hidden_two_far),
        )
        return [
            pltpu.make_async_copy(near.at[span], far.at[span], out_sems.at[step, i])
            for i, (near, far) in enumerate(pairs)
        ]

    def chunk(step, carry):
        start = pl.multiple_of(step * rows_each, rows_each)
        enc = jnp.concatenate([encode(step * FORWARD_CHUNK + q) for q in range(FORWARD_CHUNK)], axis=0)
        encoded[pl.ds(start, rows_each), :] = enc
        one = jnp.maximum(nn(enc, w_in[...]) + b_in[...], 0.0).astype(BF16)
        hidden_one[pl.ds(start, rows_each), :] = one
        two = jnp.maximum(nn(one, w_mid[...]) + b_mid[...], 0.0).astype(BF16)
        hidden_two[pl.ds(start, rows_each), :] = two
        both_heads = nt(two, w_heads[...])
        taken = dens[...]
        for q in range(FORWARD_CHUNK):
            taken = jnp.where(
                lane == FEAT + step * FORWARD_CHUNK + q, both_heads[q * BLK : (q + 1) * BLK], taken
            )
        dens[...] = taken
        for copy in leaving(step):
            copy.start()
        return carry

    lax.fori_loop(0, CAP // FORWARD_CHUNK, chunk, 0)

    pre = dens[...].T[FEAT : FEAT + CAP]
    tau = (jnp.maximum(pre, 0.0) + jnp.log1p(jnp.exp(-jnp.abs(pre)))) * STEP
    row_index = lax.broadcasted_iota(jnp.int32, (BLK, BLK), 0)
    earlier = jnp.where(row_index < lane, 1.0, 0.0).astype(BF16)
    before = folded(nn(stacked(tau, 3), earlier), 3)
    series = tau * (1.0 - tau * (0.5 - tau * (1.0 / 6.0 - tau * (1.0 / 24.0))))
    opacity = jnp.where(tau < 0.03, series, 1.0 - jnp.exp(-tau))
    weight = jnp.exp(-before) * opacity
    passed = jnp.exp(-(before + tau))
    kept[0] = weight
    kept[1] = passed
    kept[2] = jax.nn.sigmoid(pre) * STEP
    closing = [pltpu.make_async_copy(kept, kept_far, last_sems.at[REGIONS])]
    closing[0].start()
    weight_parts = stacked(weight, 2).astype(F32)
    slot_row = lax.broadcasted_iota(jnp.int32, (2 * CAP, 128), 0) & (CAP - 1)
    spread = jnp.concatenate(
        [jnp.where(slot_row == slot, weight_parts, 0.0).astype(BF16) for slot in range(CAP)],
        axis=1,
    )
    blended = folded(nn(spread, hidden_two[...]), 2)
    colour = folded(nt(stacked(blended, 2), w_heads[...]), 2)
    row8 = lax.broadcasted_iota(jnp.int32, (8, 128), 0)
    names = []
    for tile in range(CAP // 8):
        name = jnp.zeros((8, 128), F32)
        for k in range(8):
            name = jnp.where(row8 == k, rays[8 * tile + k].astype(F32), name)
        names.append(name)
    names = jnp.concatenate(names, axis=0)
    blocked = jnp.broadcast_to(1.0 - passed[:, BLK - 1 : BLK], (CAP, 128))
    closing_row = jnp.concatenate(
        [blocked, names, jnp.zeros((128 - 2 * CAP, 128), F32)], axis=0
    ).T[0:1]
    pairs = jnp.where(lane[:16] < FEAT, colour[:16], pltpu.roll(colour[16:], FEAT, 1))
    for i in range(16):
        sent[i] = pairs[i : i + 1]
    sent[16] = closing_row
    for peer in range(REGIONS):
        closing.append(
            pltpu.make_async_copy(
                sent, payload.at[pl.ds(LINES * peer, LINES)], last_sems.at[peer]
            )
        )
        closing[-1].start()
    for step in range(CAP // FORWARD_CHUNK):
        for copy in leaving(step):
            copy.wait()
    for copy in closing:
        copy.wait()


def backward_kernel(
    place,
    order,
    gathered,
    target_far,
    w_feat_far,
    w_dens_far,
    w_mid_far,
    encoded_far,
    hidden_one_far,
    hidden_two_far,
    kept_far,
    pixels,
    packed,
    target,
    w_heads,
    w_dens,
    w_mid,
    encoded,
    hidden_one,
    hidden_two,
    kept,
    chosen,
    aim,
    slopes,
    proj,
    columns,
    sum_feat,
    sum_mid,
    sum_in,
    bias_mid,
    bias_in,
    in_sems,
):
    wanted = (
        (target_far, target),
        (w_feat_far, w_heads.at[0:FEAT]),
        (w_dens_far, w_dens),
        (hidden_two_far, hidden_two),
        (kept_far, kept),
        (hidden_one_far, hidden_one),
        (encoded_far, encoded),
        (w_mid_far, w_mid),
    )
    arriving = [
        pltpu.make_async_copy(far, near, in_sems.at[i]) for i, (far, near) in enumerate(wanted)
    ]
    for copy in arriving:
        copy.start()
    rows_each = BACKWARD_CHUNK * BLK
    region = place[0]
    descending = order[0] == 1
    lane = lax.broadcasted_iota(jnp.int32, (BLK, 128), 1)

    closing_rows = jnp.concatenate(
        [gathered[LINES * j + LINES - 1] for j in range(REGIONS)], axis=0
    )
    closing_columns = jnp.concatenate(
        [closing_rows, jnp.zeros((128 - REGIONS, 128), F32)], axis=0
    ).T
    own = jnp.sum(
        jnp.where(lane[:CAP] == region, closing_columns[CAP : 2 * CAP], 0.0),
        axis=1,
        keepdims=True,
    )
    wanted = jnp.concatenate(
        [own, (lax.broadcasted_iota(jnp.int32, (8, 1), 0) + 8 * region).astype(F32)],
        axis=0,
    )
    group_of = lax.broadcasted_iota(jnp.int32, (40, 128), 1) // CAP
    for group in range(4):
        tiles = []
        names = jnp.zeros((1, 128), F32)
        for k in range(4):
            j = 4 * group + k
            pairs = gathered[LINES * j : LINES * j + 16].reshape(16, 128)
            colours = jnp.concatenate([pairs, pltpu.roll(pairs, FEAT, 1)], axis=0)
            tiles.append(jnp.where(lane[:CAP] < FEAT, colours, closing_columns[:CAP, j : j + 1]))
            turned = pltpu.roll(closing_rows[j : j + 1], (CAP * (k - 1)) % 128, 1)
            names = jnp.where(group_of[0:1] == k, turned, names)
        first, second, third = thirds(jnp.concatenate(tiles, axis=0))
        same = wanted == names
        left = jnp.concatenate(
            [jnp.where(same & (group_of == k), 1.0, 0.0).astype(BF16) for k in range(4)],
            axis=0,
        )
        found = (nn(left, third) + nn(left, second)) + nn(left, first)
        chosen[4 * group : 4 * group + 4] = found.reshape(4, 40, 128)

    position = jnp.where(descending, REGIONS - 1 - region, region)
    total = jnp.zeros((40, 128), F32)
    through = jnp.ones((40, 128), F32)
    near = jnp.ones((40, 128), F32)
    far = jnp.zeros((40, 128), F32)
    far_through = jnp.ones((40, 128), F32)
    for step in range(REGIONS):
        source = jnp.where(descending, REGIONS - 1 - step, step)
        here = chosen[source]
        through_here = 1.0 - jnp.broadcast_to(here[:, FEAT : FEAT + 1], (40, 128))
        total = total + through * here
        near = jnp.where(step < position, near * through_here, near)
        beyond = step > position
        far = jnp.where(beyond, far + far_through * here, far)
        far_through = jnp.where(beyond, far_through * through_here, far_through)
        through = through * through_here
    pixels[...] = total[32:40, :FEAT]

    for copy in arriving[:3]:
        copy.wait()
    w_heads[FEAT:128, :] = jnp.broadcast_to(w_dens[...].astype(F32), (128 - FEAT, HID)).astype(BF16)
    picked = jnp.where(own == lane[:CAP].astype(F32), 1.0, 0.0).astype(BF16)
    first, second, third = thirds(target[...])
    wished = (nt(picked, third) + nt(picked, second)) + nt(picked, first)
    wished = jnp.concatenate([wished, jnp.zeros((CAP, 128 - FEAT), F32)], axis=1)
    occupied = (own >= 0.0) & (lane[:CAP] < FEAT)
    scaled = jnp.where(occupied, near[:CAP] * (total[:CAP] - wished), 0.0)
    inner = jnp.where(occupied, scaled * far[:CAP], 0.0)
    slopes[...] = scaled
    d_through = jnp.sum(inner, axis=1, keepdims=True)
    direction = folded(nn(stacked(scaled, 3), w_heads[...]), 3)
    upper = direction.astype(BF16)
    lower = (direction - upper.astype(F32)).astype(BF16)
    aim[0:CAP, :] = upper
    aim[CAP : 2 * CAP, :] = lower
    aim[2 * CAP : 128, :] = jnp.zeros((128 - 2 * CAP, HID), BF16)

    proj[...] = jnp.zeros_like(proj)
    slot_lane = jnp.where(lane < 2 * CAP, lane & (CAP - 1), -1)

    def project(step, carry):
        start = pl.multiple_of(step * rows_each, rows_each)
        part = nt(hidden_two[pl.ds(start, rows_each), :], aim[...])
        taken = proj[...]
        for q in range(BACKWARD_CHUNK):
            taken = jnp.where(
                slot_lane == step * BACKWARD_CHUNK + q, part[q * BLK : (q + 1) * BLK], taken
            )
        proj[...] = taken
        return carry

    arriving[3].wait()
    lax.fori_loop(0, CAP // BACKWARD_CHUNK, project, 0)
    turned = proj[...].T
    projected = turned[0:CAP] + turned[CAP : 2 * CAP]
    arriving[4].wait()
    row_index = lax.broadcasted_iota(jnp.int32, (BLK, BLK), 0)
    later = jnp.where(row_index > lane, 1.0, 0.0).astype(BF16)
    weight, passed = kept[0], kept[1]
    behind = folded(nn(stacked(projected * weight, 3), later), 3)
    d_tau = projected * passed - behind - d_through * passed[:, BLK - 1 : BLK]
    columns[...] = jnp.concatenate(
        [weight, d_tau * kept[2], jnp.zeros((128 - 2 * CAP, BLK), F32)], axis=0
    ).T
    for copy in arriving[5:]:
        copy.wait()

    for ref in (sum_feat, sum_mid, sum_in, bias_mid, bias_in):
        ref[...] = jnp.zeros_like(ref)

    def chunk(step, carry):
        start = pl.multiple_of(step * rows_each, rows_each)
        turn = lax.rem(128 - step * BACKWARD_CHUNK, 128)
        here = pltpu.roll(columns[...], turn, 1)
        parts = []
        for q in range(BACKWARD_CHUNK):
            colour = slopes[pl.ds(step * BACKWARD_CHUNK + q, 1), :]
            pre_here = jnp.where(lane == FEAT, here[:, CAP + q : CAP + q + 1], 0.0)
            parts.append(jnp.where(lane < FEAT, here[:, q : q + 1] * colour, pre_here))
        d_heads = jnp.concatenate(parts, axis=0).astype(BF16)
        two = hidden_two[pl.ds(start, rows_each), :]
        one = hidden_one[pl.ds(start, rows_each), :]
        enc = encoded[pl.ds(start, rows_each), :]
        sum_feat[...] += tn(two, d_heads)
        d_two = jnp.where(two.astype(F32) > 0.0, nn(d_heads, w_heads[...]), 0.0)
        bias_mid[...] += jnp.sum(d_two.reshape(rows_each // 8, 8, HID), axis=0)
        d_two = d_two.astype(BF16)
        sum_mid[...] += tn(one, d_two)
        d_one = jnp.where(one.astype(F32) > 0.0, nt(d_two, w_mid[...]), 0.0)
        bias_in[...] += jnp.sum(d_one.reshape(rows_each // 8, 8, HID), axis=0)
        sum_in[...] += tn(enc, d_one.astype(BF16))
        return carry

    lax.fori_loop(0, CAP // BACKWARD_CHUNK, chunk, 0)

    spread = jnp.concatenate(
        [
            jnp.zeros((96, HID), F32),
            jnp.broadcast_to(jnp.sum(bias_in[...], axis=0, keepdims=True), (8, HID)),
            jnp.broadcast_to(jnp.sum(bias_mid[...], axis=0, keepdims=True), (24, HID)),
        ],
        axis=0,
    ).T
    sum_feat[...] = jnp.where(lax.broadcasted_iota(jnp.int32, (HID, 128), 1) < 96, sum_feat[...], spread)
    for part in range(BATCHES):
        packed[part, 0:8, :] = sum_mid[8 * part : 8 * part + 8, 0:128]
        packed[part, 8:16, :] = sum_mid[8 * part : 8 * part + 8, 128:256]
        packed[part, 16:20, :] = sum_in[4 * part : 4 * part + 4, 0:128]
        packed[part, 20:24, :] = sum_in[4 * part : 4 * part + 4, 128:256]
        packed[part, 24:32, :] = sum_feat[8 * part : 8 * part + 8, :]


def finish_kernel(parts, g_in, gb_in, g_mid, gb_mid, g_feat, g_dens):
    total = jnp.sum(parts[...], axis=0)
    g_mid[:, 0:128] = total[0:8]
    g_mid[:, 128:256] = total[8:16]
    g_in[:, 0:128] = total[16:20]
    g_in[:, 128:256] = total[20:24]
    g_feat[...] = total[24:32, :FEAT]
    turned = jnp.concatenate([total[24:32], jnp.zeros((120, 128), F32)], axis=0).T
    g_dens[...] = turned[FEAT : FEAT + 1, 0:8]
    gb_in[...] = turned[96:97, 0:8]
    gb_mid[...] = turned[104:105, 0:8]


VMEM = pl.BlockSpec(memory_space=pltpu.VMEM)
SMEM = pl.BlockSpec(memory_space=pltpu.SMEM)
HBM = pl.BlockSpec(memory_space=pltpu.HBM)
DMA = pltpu.SemaphoreType.DMA


def shards(
    block_rays,
    block_offsets,
    view_order,
    ray_frames,
    target,
    enc_freq,
    w_in,
    b_in,
    w_mid,
    b_mid,
    w_feat,
    w_dens,
):
    samples = CAP * BLK
    slot_rays = block_rays.reshape(CAP)
    slot_offsets = block_offsets.reshape(CAP)
    payload, *stored = pl.pallas_call(
        forward_kernel,
        name="forward",
        out_shape=(
            jax.ShapeDtypeStruct((REGIONS * LINES, 1, 128), F32),
            jax.ShapeDtypeStruct((samples, ENC), BF16),
            jax.ShapeDtypeStruct((samples, HID), BF16),
            jax.ShapeDtypeStruct((samples, HID), BF16),
            jax.ShapeDtypeStruct((3, CAP, BLK), F32),
        ),
        in_specs=[SMEM, SMEM] + [HBM] * 8,
        out_specs=(HBM,) * 5,
        scratch_shapes=[
            pltpu.VMEM((6, 1, RAYS), F32),
            pltpu.VMEM((3, 1, FEAT), F32),
            pltpu.VMEM((ENC, HID), BF16),
            pltpu.VMEM((1, HID), F32),
            pltpu.VMEM((HID, HID), BF16),
            pltpu.VMEM((1, HID), F32),
            pltpu.VMEM((128, HID), BF16),
            pltpu.VMEM((1, HID), BF16),
            pltpu.VMEM((samples, ENC), BF16),
            pltpu.VMEM((samples, HID), BF16),
            pltpu.VMEM((samples, HID), BF16),
            pltpu.VMEM((3, CAP, BLK), F32),
            pltpu.VMEM((RAYS, 128), F32),
            pltpu.VMEM((RAYS, 128), F32),
            pltpu.VMEM((BLK, 128), F32),
            pltpu.VMEM((LINES, 1, 128), F32),
            DMA((8,)),
            DMA((CAP // FORWARD_CHUNK, 3)),
            DMA((REGIONS + 1,)),
        ],
    )(
        slot_rays,
        slot_offsets,
        ray_frames.transpose(1, 0, 2),
        enc_freq.transpose(1, 0, 2),
        w_in[0],
        b_in,
        w_mid[0],
        b_mid,
        w_feat[0].T,
        w_dens,
    )
    gathered = lax.all_to_all(payload, "depth", 0, 0, tiled=True)
    place = lax.axis_index("depth").astype(jnp.int32).reshape(1)
    pixels, packed = pl.pallas_call(
        backward_kernel,
        name="backward",
        out_shape=(
            jax.ShapeDtypeStruct((8, FEAT), F32),
            jax.ShapeDtypeStruct((BATCHES, 32, 128), F32),
        ),
        in_specs=[SMEM] * 2 + [VMEM] + [HBM] * 8,
        out_specs=(VMEM,) * 2,
        scratch_shapes=[
            pltpu.VMEM((FEAT, RAYS), F32),
            pltpu.VMEM((128, HID), BF16),
            pltpu.VMEM((1, HID), BF16),
            pltpu.VMEM((HID, HID), BF16),
            pltpu.VMEM((samples, ENC), BF16),
            pltpu.VMEM((samples, HID), BF16),
            pltpu.VMEM((samples, HID), BF16),
            pltpu.VMEM((3, CAP, BLK), F32),
            pltpu.VMEM((REGIONS, 40, 128), F32),
            pltpu.VMEM((128, HID), BF16),
            pltpu.VMEM((CAP, 128), F32),
            pltpu.VMEM((BLK, 128), F32),
            pltpu.VMEM((BLK, 128), F32),
            pltpu.VMEM((HID, 128), F32),
            pltpu.VMEM((HID, HID), F32),
            pltpu.VMEM((ENC, HID), F32),
            pltpu.VMEM((8, HID), F32),
            pltpu.VMEM((8, HID), F32),
            DMA((8,)),
        ],
    )(
        place,
        view_order,
        pltpu.with_memory_space_constraint(gathered, pltpu.VMEM),
        target[0].T,
        w_feat[0].T,
        w_dens,
        w_mid[0],
        *stored,
    )
    received = lax.all_to_all(packed, "cam", 0, 0, tiled=True)
    g_in, gb_in, g_mid, gb_mid, g_feat, g_dens = pl.pallas_call(
        finish_kernel,
        name="finish",
        out_shape=(
            jax.ShapeDtypeStruct((4, HID), F32),
            jax.ShapeDtypeStruct((1, 8), F32),
            jax.ShapeDtypeStruct((8, HID), F32),
            jax.ShapeDtypeStruct((1, 8), F32),
            jax.ShapeDtypeStruct((8, FEAT), F32),
            jax.ShapeDtypeStruct((1, 8), F32),
        ),
        in_specs=[VMEM],
        out_specs=(VMEM,) * 6,
    )(pltpu.with_memory_space_constraint(received, pltpu.VMEM))
    return (pixels[None], g_in[None], gb_in, g_mid[None], gb_mid, g_feat[None], g_dens)


def solution(mesh):
    placed = (
        P("depth", "cam", None),
        P("depth", "cam", None),
        P("cam"),
        P("cam", None, None),
        P("cam", None, None),
        P("depth", None, None),
        P("depth", None, None),
        P("depth", None),
        P("depth", None, None),
        P("depth", None),
        P("depth", None, None),
        P("depth", None),
    )
    return jax.shard_map(
        shards,
        mesh=mesh,
        in_specs=placed,
        out_specs=(
            P("cam", "depth", None),
            P("depth", "cam", None),
            P("depth", "cam"),
            P("depth", "cam", None),
            P("depth", "cam"),
            P("depth", "cam", None),
            P("depth", "cam"),
        ),
        check_vma=False,
    )
```
